768 devices in a mesh: ma: 12 (over z), row: 64 (over x, y, core).
Axes of the slice: x: 4, y: 8, z: 12, core: 2. Of those that a mesh axis runs over, the one named last changes fastest.
Arguments:
- spectra: float32 [64, 3, 264, 513, 2], P('row', None, 'ma'), may hold values from -0.125 to 0.125
- legendre: bfloat16 [264, 513, 384], P('ma'), may hold values from -0.25 to 0.25
- pair_slots: int32 [264], replicated, may hold values from 0 to 263, each once
- theta_owner: int32 [384], replicated, may hold values from 0 to 383, each once
Outputs:
- flux_grid: bfloat16 [64, 768, 2, 1536], P('row', 'ma')
- flux_spectra: float32 [64, 2, 264, 513, 2], P('row', None, 'ma')
The draws below stay inside these ranges and needn't reach their ends.
Inputs may be any that keep to these rules, and one draw needn't show every extreme that they name: `pair_slots`: A value p below 256 puts the orders p and 511 - p in that slot; values of 256 or more mark empty slots. `theta_owner`: index d of ma owns the northern rows at positions d * 32 to (d + 1) * 32 - 1 and their mirror rows.
All inputs are finite; a program needn't handle non-finite values.
Results may differ from the reference program's by a relative error of at most 0.0077.
Values may be sent and summed in bfloat16 or wider, within the bound.
No kernel may reach another device: no remote copies, remote signals or barrier semaphores. Data moves between devices by JAX's collectives and lax.ppermute only.
A program may use at most 128 MiB of HBM per device.

```python
import jax
import jax.numpy as jnp
from jax import lax

LMAX = 511
NTHETA = 768
NPHI = 1536
NPAIRS = 256
PACK = 513
HALF = 384
SLOTS = 264
THETA_DEV = 64
LEVELS = 64
N_MA = 12


def block_scale(own_key, shape, split, low, largest):
    loudness = 1.0
    for position, blocks in split:
        heights = jax.random.uniform(jax.random.fold_in(jax.random.fold_in(own_key, 6), position), (blocks,), jnp.float32, low / len(split), largest / len(split))
        loudness = loudness * jnp.repeat(jnp.exp(heights), shape[position] // blocks).reshape((-1,) + (1,) * (len(shape) - 1 - position))
    return loudness


def noise(key, shape, scale, reach, cuts=(), held_as=jnp.bfloat16):
    level = block_scale(key, shape, cuts, -0.22, 0.18) if cuts else 1.0
    result = jax.random.normal(key, shape, jnp.float32) * scale * level
    return jnp.minimum(jnp.maximum(result, -reach), reach).astype(held_as)


def setup_inputs(seed: int = 0) -> dict:
    arg_keys = jax.random.split(jax.random.key(seed), 5)
    spectra = noise(arg_keys[0], (LEVELS, 3, SLOTS, PACK, 2), ((LEVELS * (LMAX + 1) // 2) ** -0.5), 0.125, ((0, 64), (2, 12)), jnp.float32)
    legendre = noise(arg_keys[1], (SLOTS, PACK, HALF), PACK ** -0.5, 0.25, ((0, 12),))
    pair_slots = jax.random.permutation(arg_keys[2], SLOTS).astype(jnp.int32)
    theta_owner = jax.random.permutation(arg_keys[3], HALF).astype(jnp.int32)
    return {"spectra": spectra, "legendre": legendre, "pair_slots": pair_slots, "theta_owner": theta_owner}


HIGH = lax.Precision.HIGHEST


def chebyshev_pair(levels):
    index = jnp.arange(levels, dtype=jnp.int32)
    products = (index[:, None] * index[None, :]) % (2 * (levels - 1))
    cosines = jnp.cos(jnp.pi * products.astype(jnp.float32) / (levels - 1))
    ends = jnp.where((index == 0) | (index == levels - 1), 0.5, 1.0).astype(jnp.float32)
    analysis = (2.0 / (levels - 1)) ** 0.5 * ends[:, None] * ends[None, :] * cosines
    return cosines, analysis


def slot_tables(pairs):
    packed = jnp.arange(PACK, dtype=jnp.int32)[None, :]
    column = pairs[:, None]
    in_use = column < NPAIRS
    low_part = in_use & (packed <= LMAX - column)
    high_part = in_use & (packed > LMAX - column)
    high_sign = 1 - 2 * ((packed + LMAX - column + 1) % 2)
    low_sign = jnp.broadcast_to(1 - 2 * (packed % 2), high_sign.shape)
    slot_masks = jnp.stack([low_part, high_part]).astype(jnp.float32)
    slot_signs = jnp.stack([low_sign, high_sign])
    even_part = slot_masks * (slot_signs > 0)
    odd_part = slot_masks * (slot_signs < 0)
    select = jnp.stack([even_part, odd_part], axis=1)
    orders = jnp.stack([pairs, LMAX - pairs], axis=1)
    return select, orders


def fourier_tables(orders):
    points = jnp.arange(NPHI, dtype=jnp.int32)
    phase = (orders[:, :, None] * points[None, None, :]) % NPHI
    angles = 2.0 * jnp.pi * phase.astype(jnp.float32) / NPHI
    weight = jnp.where(orders == 0, 1.0, 2.0).astype(jnp.float32)[:, :, None]
    synth_tab = jnp.stack([weight * jnp.cos(angles), -weight * jnp.sin(angles)]).astype(jnp.bfloat16)
    analysis_tab = jnp.stack([jnp.cos(angles), -jnp.sin(angles)]).astype(jnp.bfloat16)
    return synth_tab, analysis_tab


def reference(spectra, legendre, pair_slots, theta_owner):
    synth_mat, analysis_mat = chebyshev_pair(LEVELS)
    level_sums = jnp.einsum("kn,nfsjc->kfsjc", synth_mat, spectra, precision=HIGH)
    level_coeffs = level_sums.astype(jnp.bfloat16)
    select, orders = slot_tables(pair_slots)
    synth_tab, analysis_tab = fourier_tables(orders)
    synth_wide = synth_tab.astype(jnp.float32)
    analysis_wide = analysis_tab.astype(jnp.float32)
    table_wide = legendre.astype(jnp.float32)
    own_half = THETA_DEV // 2

    def to_owner(values):
        return values[..., theta_owner].reshape(values.shape[:-1] + (N_MA, own_half))

    def level_pass(coeffs):
        halves = jnp.einsum("fsjc,vesj,sji->fcsvei", coeffs.astype(jnp.float32), select, table_wide, precision=HIGH)
        north_rows = (halves[:, :, :, :, 0] + halves[:, :, :, :, 1]).astype(jnp.bfloat16)
        south_rows = (halves[:, :, :, :, 0] - halves[:, :, :, :, 1]).astype(jnp.bfloat16)
        rows = jnp.stack([to_owner(north_rows), to_owner(south_rows)], axis=-2)
        rows = rows.reshape(north_rows.shape[:-1] + (NTHETA,))
        grid_vals = jnp.einsum("fcsvt,csvp->ftp", rows.astype(jnp.float32), synth_wide, precision=HIGH)
        flux_vals = (grid_vals[0:1] * grid_vals[1:3]).astype(jnp.bfloat16)
        fourier = jnp.einsum("gtp,csvp->gcsvt", flux_vals.astype(jnp.float32), analysis_wide, precision=HIGH) * NPHI ** -0.5
        split_rows = fourier.reshape(fourier.shape[:-1] + (N_MA, 2, own_half))
        north_own = split_rows[..., 0, :].reshape(fourier.shape[:-1] + (HALF,))
        south_own = split_rows[..., 1, :].reshape(fourier.shape[:-1] + (HALF,))
        base = jnp.zeros(fourier.shape[:-1] + (HALF,), jnp.float32)
        north_nat = base.at[..., theta_owner].set(north_own)
        south_nat = base.at[..., theta_owner].set(south_own)
        parity_sums = jnp.stack([north_nat + south_nat, north_nat - south_nat])
        spectral = jnp.einsum("egcsvi,sji,vesj->gsjc", parity_sums, table_wide, select, precision=HIGH)
        return jnp.transpose(flux_vals, (1, 0, 2)), spectral

    flux_grid, spectral = lax.map(level_pass, level_coeffs)
    flux_spectra = jnp.einsum("nk,kgsjc->ngsjc", analysis_mat, spectral, precision=HIGH)
    return flux_grid, flux_spectra
```

```python
import math

import jax
import jax.numpy as jnp
import numpy as np
from jax import lax
from jax.experimental import pallas as pl
from jax.experimental.pallas import tpu as pltpu
from jax.sharding import PartitionSpec as P

LMAX = 511
NPHI = 1536
NPAIRS = 256
PACK = 513
LANES = 128
TILES = -(-PACK // LANES)
FULL = PACK // LANES * LANES
BF16 = jnp.bfloat16
F32 = jnp.float32
HIGH = lax.Precision.HIGHEST
NT = (((1,), (1,)), ((), ()))


def chebyshev_pair(levels):
    index = np.arange(levels)
    cosines = np.cos(np.pi * (np.outer(index, index) % (2 * (levels - 1))) / (levels - 1))
    ends = np.where((index == 0) | (index == levels - 1), 0.5, 1.0)
    analysis = (2.0 / (levels - 1)) ** 0.5 * np.outer(ends, ends) * cosines
    return cosines.astype(np.float32), analysis.astype(np.float32)


def one_hot(theta_row):
    half = theta_row.shape[1]
    natural = lax.broadcasted_iota(jnp.int32, (half, half), 0)
    return jnp.where(natural == theta_row, 1.0, 0.0).astype(BF16)


def pack_kernel(spectra_ref, out_ref):
    pairs = spectra_ref.shape[0]
    lane = lax.broadcasted_iota(jnp.int32, (2, LANES), 1)
    for i in range(pairs):
        for j in range(TILES - 1):
            out_ref[i * TILES + j] = spectra_ref[i, :, j * LANES : (j + 1) * LANES].astype(BF16)
        last = jnp.broadcast_to(spectra_ref[i, :, FULL:PACK], (2, LANES))
        out_ref[i * TILES + TILES - 1] = jnp.where(lane == 0, last, 0.0).astype(BF16)
    for t in range(pairs * TILES, out_ref.shape[0]):
        out_ref[t] = jnp.zeros((2, LANES), BF16)


def unpack_kernel(tiles_ref, out_ref):
    for i in range(out_ref.shape[0]):
        for j in range(TILES - 1):
            out_ref[i, :, j * LANES : (j + 1) * LANES] = tiles_ref[i * TILES + j].astype(F32)
        out_ref[i, :, FULL:PACK] = tiles_ref[i * TILES + TILES - 1].astype(F32)[:, 0:1]


def slot_masks(pair, column, order_odd):
    used = pair < NPAIRS
    low = jnp.where(used & (column <= LMAX - pair), 1.0, 0.0)
    high = jnp.where(used & (column > LMAX - pair), 1.0, 0.0)
    low_sign = (1 - 2 * (column & 1)).astype(F32)
    high_sign = (1 - 2 * ((column + pair) & 1)).astype(F32)
    return jnp.where(order_odd, high, low), jnp.where(order_odd, high_sign, low_sign)


def synthesis_kernel(pairs_ref, where_ref, tiles_ref, table_ref, theta_ref, out_ref, rows_ref):
    step = pl.program_id(0)
    slots = pl.num_programs(0)
    count = tiles_ref.shape[0]
    owners = out_ref.shape[0]
    own_half = theta_ref.shape[1] // owners
    slot_dev = rows_ref.shape[1] // 24
    pair = pairs_ref[where_ref[0] * slot_dev + step]
    row = lax.broadcasted_iota(jnp.int32, (8, LANES), 0)
    odd = (row & 1) == 1
    field = row >> 1
    lane = lax.broadcasted_iota(jnp.int32, (8, LANES), 1)
    weight = jnp.where((pair == 0) & (row & 1 == 0), 1.0, 2.0)
    blocks = [[], [], [], []]
    for j in range(TILES):
        tiles = [tiles_ref[(f * slot_dev + step) * TILES + j].astype(F32) for f in range(3)]
        mask, sign = slot_masks(pair, lane + j * LANES, odd)
        mask = mask * weight
        for c in range(2):
            parts = [jnp.broadcast_to(t[c : c + 1], (8, LANES)) for t in tiles]
            base = jnp.where(field == 0, parts[0], jnp.where(field == 1, parts[1], parts[2]))
            base = base * mask
            blocks[2 * c].append(base)
            blocks[2 * c + 1].append(base * sign)
    left = jnp.concatenate([jnp.concatenate(b, axis=1) for b in blocks], axis=0)
    sums = jnp.dot(left[:, :FULL].astype(BF16), table_ref[0, :FULL, :], preferred_element_type=F32)
    sums = sums + left[:, FULL : FULL + 1] * table_ref[0, FULL:PACK, :].astype(F32)
    sums = sums.astype(BF16).astype(F32)
    for k in range(4):
        for g in range(rows_ref.shape[0]):
            rows_ref[g, pl.ds(k * 6 * slot_dev + step, 6, stride=slot_dev), :] = sums[
                k * 8 : k * 8 + 6, g * LANES : (g + 1) * LANES
            ]

    @pl.when(step == slots - 1)
    def _():
        select = one_hot(theta_ref[...])
        block = 6 * slot_dev
        moved = []
        for k in range(4):
            rows = jnp.concatenate(
                [rows_ref[g, k * block : (k + 1) * block, :] for g in range(rows_ref.shape[0])],
                axis=1,
            ).astype(BF16)
            moved.append(jnp.dot(rows, select, preferred_element_type=F32))
        for d in range(owners):
            out_ref[d] = jnp.concatenate(
                [m[:, d * own_half : (d + 1) * own_half] for m in moved], axis=1
            ).astype(BF16)


def table_kernel(coarse_cos_ref, coarse_sin_ref, fine_cos_ref, fine_sin_ref, out_ref):
    rows = fine_cos_ref.shape[0]
    fine_cos = fine_cos_ref[...]
    fine_sin = fine_sin_ref[...]
    for a in range(NPHI // LANES):
        cos_a = coarse_cos_ref[:, a : a + 1]
        sin_a = coarse_sin_ref[:, a : a + 1]
        span = slice(a * LANES, (a + 1) * LANES)
        out_ref[0, :, span] = (cos_a * fine_cos - sin_a * fine_sin).astype(BF16)
        out_ref[1, :, span] = (-(sin_a * fine_cos + cos_a * fine_sin)).astype(BF16)


def fourier_kernel(rows_ref, table_ref, flux_ref, out_ref, left_ref, sum_ref):
    step = pl.program_id(0)
    owners = rows_ref.shape[0]
    part = rows_ref.shape[1] // 3
    theta = rows_ref.shape[2] // 2

    @pl.when(step == 0)
    def _():
        turned = [rows_ref[d].astype(F32).T for d in range(owners)]
        for f in range(3):
            for c in range(2):
                left_ref[c, f * theta : (f + 1) * theta, :] = jnp.concatenate(
                    [t[c * theta : (c + 1) * theta, f * part : (f + 1) * part] for t in turned],
                    axis=1,
                ).astype(BF16)
        sum_ref[...] = jnp.zeros_like(sum_ref)

    grid = jnp.dot(left_ref[0], table_ref[0], preferred_element_type=F32)
    grid = grid + jnp.dot(left_ref[1], table_ref[1], preferred_element_type=F32)
    flux = [(grid[:theta] * grid[(1 + g) * theta : (2 + g) * theta]).astype(BF16) for g in range(2)]
    for g in range(2):
        flux_ref[g] = flux[g]
    both = jnp.concatenate(flux, axis=0)
    for c in range(2):
        sum_ref[c] += lax.dot_general(table_ref[c], both, NT, preferred_element_type=F32)

    @pl.when(step == pl.num_programs(0) - 1)
    def _():
        for d in range(owners):
            out_ref[d] = (
                jnp.concatenate([sum_ref[c, d * part : (d + 1) * part, :] for c in range(2)], axis=0)
                * NPHI ** (-0.5)
            ).astype(BF16)


def analysis_kernel(pairs_ref, where_ref, rows_ref, table_ref, theta_ref, out_ref, nat_ref):
    step = pl.program_id(0)
    owners = rows_ref.shape[0]
    own_half = theta_ref.shape[1] // owners
    block = rows_ref.shape[1]
    slot_dev = block // 4
    groups = nat_ref.shape[0]

    @pl.when(step == 0)
    def _():
        select = one_hot(theta_ref[...])
        wide = [rows_ref[d].astype(F32) for d in range(owners)]
        for k in range(4):
            own = jnp.concatenate([w[:, k * own_half : (k + 1) * own_half] for w in wide], axis=1)
            nat = lax.dot_general(own.astype(BF16), select, NT, preferred_element_type=F32)
            for g in range(groups):
                nat_ref[g, k * block : (k + 1) * block, :] = nat[:, g * LANES : (g + 1) * LANES]
        for t in range(2 * slot_dev * TILES, out_ref.shape[0]):
            out_ref[t] = jnp.zeros((2, LANES), BF16)

    left = jnp.concatenate(
        [nat_ref[g, pl.ds(step, 16, stride=slot_dev), :] for g in range(groups)], axis=1
    )
    sums = lax.dot_general(
        left.astype(BF16), table_ref[0, :FULL, :], NT, preferred_element_type=F32
    )
    last = jnp.sum(left * table_ref[0, FULL:PACK, :].astype(F32), axis=1, keepdims=True)
    pair = pairs_ref[where_ref[0] * slot_dev + step]
    row = lax.broadcasted_iota(jnp.int32, (16, LANES), 0)
    odd = (row & 1) == 1
    south = (row & 4) == 4
    lane = lax.broadcasted_iota(jnp.int32, (16, LANES), 1)
    for j in range(TILES):
        mask, sign = slot_masks(pair, lane + j * LANES, odd)
        if j < TILES - 1:
            part = sums[:, j * LANES : (j + 1) * LANES]
        else:
            part = jnp.where(lane == 0, last, 0.0)
        part = part * mask * jnp.where(south, sign, 1.0)
        for g in range(2):
            both = part[g * 8 : g * 8 + 4] + part[g * 8 + 4 : g * 8 + 8]
            tile = jnp.concatenate([both[0:1] + both[1:2], both[2:3] + both[3:4]], axis=0)
            out_ref[(g * slot_dev + step) * TILES + j] = tile.astype(BF16)


def whole(shape):
    return pl.BlockSpec(shape, lambda *_: (0,) * len(shape))


def level_mix(tiles, matrix):
    levels = matrix.shape[0]
    share = tiles.shape[0] // levels
    here = lax.all_to_all(tiles, "row", split_axis=0, concat_axis=0, tiled=True)
    here = here.reshape(levels, share * 2 * LANES).astype(F32)
    mixed = jnp.dot(matrix, here, precision=HIGH).astype(BF16)
    mixed = mixed.reshape(levels * share, 2, LANES)
    return lax.all_to_all(mixed, "row", split_axis=0, concat_axis=0, tiled=True)


def trig_table(pair_slots, owners, slot_dev):
    pairs = pair_slots.reshape(owners, 1, slot_dev)
    orders = jnp.concatenate([pairs, LMAX - pairs], axis=1).reshape(-1, 1)
    span = lax.broadcasted_iota(jnp.int32, (1, LANES), 1)
    coarse = (orders * (span * LANES)) % NPHI
    fine = (orders * span) % NPHI
    scale = 2.0 * math.pi / NPHI
    coarse = coarse.astype(F32) * scale
    fine = fine.astype(F32) * scale
    rows = orders.shape[0]
    return pl.pallas_call(
        table_kernel,
        out_shape=jax.ShapeDtypeStruct((2, rows, NPHI), BF16),
        name="table",
    )(jnp.cos(coarse), jnp.sin(coarse), jnp.cos(fine), jnp.sin(fine))


def local(spectra, legendre, pair_slots, theta_owner):
    slot_dev, _, half = legendre.shape
    owners = lax.axis_size("ma")
    levels = lax.axis_size("row") * spectra.shape[0]
    theta_dev = 2 * half // owners
    groups = half // LANES
    synth_mat, analysis_mat = chebyshev_pair(levels)
    where = lax.axis_index("ma").astype(jnp.int32).reshape(1)
    theta_row = theta_owner.reshape(1, half)
    table = trig_table(pair_slots, owners, slot_dev)

    flat = jnp.transpose(spectra, (0, 1, 2, 4, 3)).reshape(3 * slot_dev, 2, PACK)
    share = -(-3 * slot_dev * TILES // levels)
    tiles = pl.pallas_call(
        pack_kernel,
        out_shape=jax.ShapeDtypeStruct((share * levels, 2, LANES), BF16),
        name="pack",
    )(flat)
    tiles = level_mix(tiles, synth_mat)

    slot_block = pl.BlockSpec((1, PACK, half), lambda s, *_: (s, 0, 0))
    outgoing = pl.pallas_call(
        synthesis_kernel,
        out_shape=jax.ShapeDtypeStruct((owners, 6 * slot_dev, LANES), BF16),
        grid_spec=pltpu.PrefetchScalarGridSpec(
            num_scalar_prefetch=2,
            grid=(slot_dev,),
            in_specs=[whole(tiles.shape), slot_block, whole(theta_row.shape)],
            out_specs=whole((owners, 6 * slot_dev, LANES)),
            scratch_shapes=[pltpu.VMEM((groups, 24 * slot_dev, LANES), F32)],
        ),
        name="synthesis",
    )(pair_slots, where, tiles, legendre, theta_row)
    rows = lax.all_to_all(outgoing, "ma", split_axis=0, concat_axis=0, tiled=True)

    width = 256
    orders = table.shape[1]
    flux, fourier = pl.pallas_call(
        fourier_kernel,
        out_shape=(
            jax.ShapeDtypeStruct((2, theta_dev, NPHI), BF16),
            jax.ShapeDtypeStruct((owners, 4 * slot_dev, 2 * theta_dev), BF16),
        ),
        grid=(NPHI // width,),
        in_specs=[whole(rows.shape), pl.BlockSpec((2, orders, width), lambda q: (0, 0, q))],
        out_specs=(
            pl.BlockSpec((2, theta_dev, width), lambda q: (0, 0, q)),
            whole((owners, 4 * slot_dev, 2 * theta_dev)),
        ),
        scratch_shapes=[
            pltpu.VMEM((2, 3 * theta_dev, orders), BF16),
            pltpu.VMEM((2, orders, 2 * theta_dev), F32),
        ],
        name="fourier",
    )(rows, table)
    returned = lax.all_to_all(fourier, "ma", split_axis=0, concat_axis=0, tiled=True)

    share = -(-2 * slot_dev * TILES // levels)
    tiles = pl.pallas_call(
        analysis_kernel,
        out_shape=jax.ShapeDtypeStruct((share * levels, 2, LANES), BF16),
        grid_spec=pltpu.PrefetchScalarGridSpec(
            num_scalar_prefetch=2,
            grid=(slot_dev,),
            in_specs=[whole(returned.shape), slot_block, whole(theta_row.shape)],
            out_specs=whole((share * levels, 2, LANES)),
            scratch_shapes=[pltpu.VMEM((groups, 16 * slot_dev, LANES), F32)],
        ),
        name="analysis",
    )(pair_slots, where, returned, legendre, theta_row)
    tiles = level_mix(tiles, analysis_mat)
    result = pl.pallas_call(
        unpack_kernel,
        out_shape=jax.ShapeDtypeStruct((2 * slot_dev, 2, PACK), F32),
        name="unpack",
    )(tiles)
    result = jnp.transpose(result.reshape(1, 2, slot_dev, 2, PACK), (0, 1, 2, 4, 3))
    return jnp.transpose(flux, (1, 0, 2))[None], result


def solution(mesh):
    in_specs = (P("row", None, "ma", None, None), P("ma", None, None), P(), P())
    out_specs = (P("row", "ma", None, None), P("row", None, "ma", None, None))
    return jax.shard_map(local, mesh=mesh, in_specs=in_specs, out_specs=out_specs, check_vma=False)
```

```python
import math

import jax
import jax.numpy as jnp
import numpy as np
from jax import lax
from jax.experimental import pallas as pl
from jax.experimental.pallas import tpu as pltpu
from jax.sharding import PartitionSpec as P

LMAX = 511
NPHI = 1536
NPAIRS = 256
PACK = 513
LANES = 128
TILES = -(-PACK // LANES)
FULL = PACK // LANES * LANES
WIDTH = 256
SCOPED = 24 << 20
BF16 = jnp.bfloat16
F32 = jnp.float32
HIGH = lax.Precision.HIGHEST
NT = (((1,), (1,)), ((), ()))


def chebyshev_pair(levels):
    index = np.arange(levels)
    cosines = np.cos(np.pi * (np.outer(index, index) % (2 * (levels - 1))) / (levels - 1))
    ends = np.where((index == 0) | (index == levels - 1), 0.5, 1.0)
    analysis = (2.0 / (levels - 1)) ** 0.5 * np.outer(ends, ends) * cosines
    return cosines.astype(np.float32), analysis.astype(np.float32)


def one_hot(theta_row):
    half = theta_row.shape[1]
    natural = lax.broadcasted_iota(jnp.int32, (half, half), 0)
    return jnp.where(natural == theta_row, 1.0, 0.0).astype(BF16)


def pack_kernel(spectra_ref, out_ref):
    pairs = spectra_ref.shape[0]
    lane = lax.broadcasted_iota(jnp.int32, (2, LANES), 1)
    for i in range(pairs):
        for j in range(TILES - 1):
            out_ref[i * TILES + j] = spectra_ref[i, :, j * LANES : (j + 1) * LANES].astype(BF16)
        last = jnp.broadcast_to(spectra_ref[i, :, FULL:PACK], (2, LANES))
        out_ref[i * TILES + TILES - 1] = jnp.where(lane == 0, last, 0.0).astype(BF16)
    for t in range(pairs * TILES, out_ref.shape[0]):
        out_ref[t] = jnp.zeros((2, LANES), BF16)


def unpack_kernel(tiles_ref, out_ref):
    for i in range(out_ref.shape[0]):
        for j in range(TILES - 1):
            out_ref[i, :, j * LANES : (j + 1) * LANES] = tiles_ref[i * TILES + j].astype(F32)
        out_ref[i, :, FULL:PACK] = tiles_ref[i * TILES + TILES - 1].astype(F32)[:, 0:1]


def slot_masks(pair, column, order_odd):
    used = pair < NPAIRS
    low = jnp.where(used & (column <= LMAX - pair), 1.0, 0.0)
    high = jnp.where(used & (column > LMAX - pair), 1.0, 0.0)
    low_sign = (1 - 2 * (column & 1)).astype(F32)
    high_sign = (1 - 2 * ((column + pair) & 1)).astype(F32)
    return jnp.where(order_odd, high, low), jnp.where(order_odd, high_sign, low_sign)


def slot_copy(source_ref, table_ref, arrived, slot):
    return pltpu.make_async_copy(source_ref.at[slot], table_ref.at[slot], arrived.at[slot])


def synthesis_kernel(
    pairs_ref, where_ref, source_ref, tiles_ref, theta_ref, out_ref, rows_ref, table_ref, arrived
):
    slots = table_ref.shape[0]
    for slot in range(slots):
        slot_copy(source_ref, table_ref, arrived, slot).start()
    owners = out_ref.shape[0]
    own_half = theta_ref.shape[1] // owners
    groups = rows_ref.shape[0]
    block = 6 * slots
    row = lax.broadcasted_iota(jnp.int32, (8, LANES), 0)
    odd = (row & 1) == 1
    field = row >> 1
    lane = lax.broadcasted_iota(jnp.int32, (8, LANES), 1)

    def one_slot(slot, carry):
        pair = pairs_ref[where_ref[0] * slots + slot]
        weight = jnp.where((pair == 0) & (row & 1 == 0), 1.0, 2.0)
        blocks = [[], [], [], []]
        for j in range(TILES):
            tiles = [tiles_ref[(f * slots + slot) * TILES + j].astype(F32) for f in range(3)]
            mask, sign = slot_masks(pair, lane + j * LANES, odd)
            mask = mask * weight
            for c in range(2):
                parts = [jnp.broadcast_to(t[c : c + 1], (8, LANES)) for t in tiles]
                base = jnp.where(field == 0, parts[0], jnp.where(field == 1, parts[1], parts[2]))
                base = base * mask
                blocks[2 * c].append(base)
                blocks[2 * c + 1].append(base * sign)
        left = jnp.concatenate([jnp.concatenate(b, axis=1) for b in blocks], axis=0)
        slot_copy(source_ref, table_ref, arrived, slot).wait()
        sums = jnp.dot(
            left[:, :FULL].astype(BF16), table_ref[slot, :FULL, :], preferred_element_type=F32
        )
        sums = sums + left[:, FULL : FULL + 1] * table_ref[slot, FULL:PACK, :].astype(F32)
        for k in range(4):
            for g in range(groups):
                rows_ref[g, pl.ds(k * block + slot, 6, stride=slots), :] = sums[
                    k * 8 : k * 8 + 6, g * LANES : (g + 1) * LANES
                ]
        return carry

    lax.fori_loop(0, slots, one_slot, None, unroll=2)
    select = one_hot(theta_ref[...])
    moved = []
    for k in range(4):
        rows = jnp.concatenate(
            [rows_ref[g, k * block : (k + 1) * block, :] for g in range(groups)], axis=1
        ).astype(BF16)
        moved.append(jnp.dot(rows, select, preferred_element_type=F32))
    for d in range(owners):
        out_ref[d] = jnp.concatenate(
            [m[:, d * own_half : (d + 1) * own_half] for m in moved], axis=1
        ).astype(BF16)


def table_kernel(coarse_cos_ref, coarse_sin_ref, fine_cos_ref, fine_sin_ref, out_ref):
    rows = fine_cos_ref.shape[0]
    fine_cos = fine_cos_ref[...]
    fine_sin = fine_sin_ref[...]
    for a in range(NPHI // LANES):
        cos_a = coarse_cos_ref[:, a : a + 1]
        sin_a = coarse_sin_ref[:, a : a + 1]
        span = slice(a * LANES, (a + 1) * LANES)
        out_ref[:rows, span] = (cos_a * fine_cos - sin_a * fine_sin).astype(BF16)
        out_ref[rows:, span] = (-(sin_a * fine_cos + cos_a * fine_sin)).astype(BF16)


def fourier_kernel(rows_ref, table_ref, flux_ref, out_ref, left_ref, both_ref, sum_ref):
    owners = rows_ref.shape[0]
    part = rows_ref.shape[1] // 3
    theta = rows_ref.shape[2] // 2
    orders = owners * part
    wide = [rows_ref[d].astype(F32) for d in range(owners)]
    for f in range(3):
        turned = jnp.concatenate([w[f * part : (f + 1) * part] for w in wide], axis=0).T
        left_ref[f * theta : (f + 1) * theta, :] = jnp.concatenate(
            [turned[:theta], turned[theta:]], axis=1
        ).astype(BF16)
    for q in range(NPHI // WIDTH):
        span = slice(q * WIDTH, (q + 1) * WIDTH)
        grid = jnp.dot(left_ref[...], table_ref[:, span], preferred_element_type=F32)
        for g in range(2):
            flux = (grid[:theta] * grid[(1 + g) * theta : (2 + g) * theta]).astype(BF16)
            flux_ref[g, :, span] = flux
            both_ref[g * theta : (g + 1) * theta, span] = flux
    sum_ref[...] = lax.dot_general(
        table_ref[...], both_ref[...], NT, preferred_element_type=F32
    ) * NPHI ** (-0.5)
    for d in range(owners):
        out_ref[d] = jnp.concatenate(
            [sum_ref[c * orders + d * part : c * orders + (d + 1) * part, :] for c in range(2)],
            axis=0,
        ).astype(BF16)


def analysis_kernel(
    pairs_ref, where_ref, source_ref, rows_ref, theta_ref, out_ref, nat_ref, table_ref, arrived
):
    slots = table_ref.shape[0]
    for slot in range(slots):
        slot_copy(source_ref, table_ref, arrived, slot).start()
    owners = rows_ref.shape[0]
    own_half = theta_ref.shape[1] // owners
    block = rows_ref.shape[1]
    groups = nat_ref.shape[0]
    select = one_hot(theta_ref[...])
    wide = [rows_ref[d].astype(F32) for d in range(owners)]
    for k in range(4):
        own = jnp.concatenate([w[:, k * own_half : (k + 1) * own_half] for w in wide], axis=1)
        nat = lax.dot_general(own.astype(BF16), select, NT, preferred_element_type=F32)
        for g in range(groups):
            nat_ref[g, k * block : (k + 1) * block, :] = nat[:, g * LANES : (g + 1) * LANES]
    for t in range(2 * slots * TILES, out_ref.shape[0]):
        out_ref[t] = jnp.zeros((2, LANES), BF16)
    row = lax.broadcasted_iota(jnp.int32, (16, LANES), 0)
    odd = (row & 1) == 1
    south = (row & 4) == 4
    lane = lax.broadcasted_iota(jnp.int32, (16, LANES), 1)

    def one_slot(slot, carry):
        left = jnp.concatenate(
            [nat_ref[g, pl.ds(slot, 16, stride=slots), :] for g in range(groups)], axis=1
        )
        slot_copy(source_ref, table_ref, arrived, slot).wait()
        sums = lax.dot_general(
            left.astype(BF16), table_ref[slot, :FULL, :], NT, preferred_element_type=F32
        )
        last = jnp.sum(left * table_ref[slot, FULL:PACK, :].astype(F32), axis=1, keepdims=True)
        pair = pairs_ref[where_ref[0] * slots + slot]
        for j in range(TILES):
            mask, sign = slot_masks(pair, lane + j * LANES, odd)
            if j < TILES - 1:
                part = sums[:, j * LANES : (j + 1) * LANES]
            else:
                part = jnp.where(lane == 0, last, 0.0)
            part = part * mask * jnp.where(south, sign, 1.0)
            for g in range(2):
                both = part[g * 8 : g * 8 + 4] + part[g * 8 + 4 : g * 8 + 8]
                tile = jnp.concatenate([both[0:1] + both[1:2], both[2:3] + both[3:4]], axis=0)
                out_ref[(g * slots + slot) * TILES + j] = tile.astype(BF16)
        return carry

    lax.fori_loop(0, slots, one_slot, None, unroll=2)


def call(kernel, name, out_shape, operands, scratch=(), scalars=0, remote=0):
    first = scalars + remote
    spaces = [pltpu.SMEM] * scalars + [pltpu.HBM] * remote + [pltpu.VMEM] * (len(operands) - first)
    operands = [
        x if i < first else pltpu.with_memory_space_constraint(x, pltpu.VMEM)
        for i, x in enumerate(operands)
    ]
    return pl.pallas_call(
        kernel,
        out_shape=tuple(pltpu.VMEM(shape, dtype) for shape, dtype in out_shape),
        in_specs=[pl.BlockSpec(memory_space=space) for space in spaces],
        out_specs=(pl.BlockSpec(memory_space=pltpu.VMEM),) * len(out_shape),
        scratch_shapes=scratch,
        compiler_params=pltpu.CompilerParams(vmem_limit_bytes=SCOPED),
        name=name,
    )(*operands)


def level_mix(tiles, matrix, beside=None):
    levels = matrix.shape[0]
    share = tiles.shape[0] // levels
    here = lax.all_to_all(tiles, "row", split_axis=0, concat_axis=0, tiled=True)
    here, beside = lax.optimization_barrier((here, beside))
    here = here.reshape(levels, share * 2 * LANES).astype(F32)
    mixed = jnp.dot(matrix, here, precision=HIGH).astype(BF16)
    mixed = mixed.reshape(levels * share, 2, LANES)
    return lax.all_to_all(mixed, "row", split_axis=0, concat_axis=0, tiled=True), beside


def trig_table(pair_slots, owners, slot_dev):
    pairs = pair_slots.reshape(owners, 1, slot_dev)
    orders = jnp.concatenate([pairs, LMAX - pairs], axis=1).reshape(-1, 1)
    span = lax.broadcasted_iota(jnp.int32, (1, LANES), 1)
    coarse = (orders * (span * LANES)) % NPHI
    fine = (orders * span) % NPHI
    scale = 2.0 * math.pi / NPHI
    coarse = coarse.astype(F32) * scale
    fine = fine.astype(F32) * scale
    shape = (2 * orders.shape[0], NPHI)
    trig = (jnp.cos(coarse), jnp.sin(coarse), jnp.cos(fine), jnp.sin(fine))
    return call(table_kernel, "table", [(shape, BF16)], trig)[0]


def local(spectra, legendre, pair_slots, theta_owner):
    slot_dev, _, half = legendre.shape
    owners = lax.axis_size("ma")
    levels = lax.axis_size("row") * spectra.shape[0]
    theta_dev = 2 * half // owners
    groups = half // LANES
    synth_mat, analysis_mat = chebyshev_pair(levels)
    where = lax.axis_index("ma").astype(jnp.int32).reshape(1)
    theta_row = theta_owner.reshape(1, half)
    table = trig_table(pair_slots, owners, slot_dev)

    held = [pltpu.VMEM(legendre.shape, BF16), pltpu.SemaphoreType.DMA((slot_dev,))]
    flat = jnp.transpose(spectra, (0, 1, 2, 4, 3)).reshape(3 * slot_dev, 2, PACK)
    share = -(-3 * slot_dev * TILES // levels)
    (tiles,) = pl.pallas_call(
        pack_kernel,
        out_shape=(pltpu.VMEM((share * levels, 2, LANES), BF16),),
        out_specs=(pl.BlockSpec(memory_space=pltpu.VMEM),),
        compiler_params=pltpu.CompilerParams(vmem_limit_bytes=SCOPED),
        name="pack",
    )(flat)
    tiles, (table, theta_row) = level_mix(tiles, synth_mat, (table, theta_row))

    (outgoing,) = call(
        synthesis_kernel,
        "synthesis",
        [((owners, 6 * slot_dev, LANES), BF16)],
        (pair_slots, where, legendre, tiles, theta_row),
        [pltpu.VMEM((groups, 24 * slot_dev, LANES), F32)] + held,
        scalars=2,
        remote=1,
    )
    rows = lax.all_to_all(outgoing, "ma", split_axis=0, concat_axis=0, tiled=True)

    orders = table.shape[0]
    flux, fourier = call(
        fourier_kernel,
        "fourier",
        [((2, theta_dev, NPHI), BF16), ((owners, 4 * slot_dev, 2 * theta_dev), BF16)],
        (rows, table),
        [
            pltpu.VMEM((3 * theta_dev, orders), BF16),
            pltpu.VMEM((2 * theta_dev, NPHI), BF16),
            pltpu.VMEM((orders, 2 * theta_dev), F32),
        ],
    )
    returned = lax.all_to_all(fourier, "ma", split_axis=0, concat_axis=0, tiled=True)

    share = -(-2 * slot_dev * TILES // levels)
    (tiles,) = call(
        analysis_kernel,
        "analysis",
        [((share * levels, 2, LANES), BF16)],
        (pair_slots, where, legendre, returned, theta_row),
        [pltpu.VMEM((groups, 16 * slot_dev, LANES), F32)] + held,
        scalars=2,
        remote=1,
    )
    flux = jnp.transpose(flux, (1, 0, 2))[None]
    tiles, flux = level_mix(tiles, analysis_mat, flux)
    tiles = pltpu.with_memory_space_constraint(tiles, pltpu.VMEM)
    result = pl.pallas_call(
        unpack_kernel,
        out_shape=jax.ShapeDtypeStruct((2 * slot_dev, 2, PACK), F32),
        in_specs=[pl.BlockSpec(memory_space=pltpu.VMEM)],
        compiler_params=pltpu.CompilerParams(vmem_limit_bytes=SCOPED),
        name="unpack",
    )(tiles)
    result = jnp.transpose(result.reshape(1, 2, slot_dev, 2, PACK), (0, 1, 2, 4, 3))
    return flux, result


def solution(mesh):
    in_specs = (P("row", None, "ma", None, None), P("ma", None, None), P(), P())
    out_specs = (P("row", "ma", None, None), P("row", None, "ma", None, None))
    return jax.shard_map(local, mesh=mesh, in_specs=in_specs, out_specs=out_specs, check_vma=False)
```

```python
import math

import jax
import jax.numpy as jnp
import numpy as np
from jax import lax
from jax.experimental import pallas as pl
from jax.experimental.pallas import tpu as pltpu
from jax.sharding import PartitionSpec as P

LMAX = 511
NPHI = 1536
NPAIRS = 256
PACK = 513
LANES = 128
TILES = -(-PACK // LANES)
FULL = PACK // LANES * LANES
WIDTH = 256
SCOPED = 16 << 20
SYNTHESIS_SCOPED = 46 << 20
GROUP = 4
BF16 = jnp.bfloat16
F32 = jnp.float32
HIGH = lax.Precision.HIGHEST
NT = (((1,), (1,)), ((), ()))


def chebyshev_pair(levels):
    index = np.arange(levels)
    cosines = np.cos(np.pi * (np.outer(index, index) % (2 * (levels - 1))) / (levels - 1))
    ends = np.where((index == 0) | (index == levels - 1), 0.5, 1.0)
    analysis = (2.0 / (levels - 1)) ** 0.5 * np.outer(ends, ends) * cosines
    return cosines.astype(np.float32), analysis.astype(np.float32)


def one_hot(theta_row):
    half = theta_row.shape[1]
    natural = lax.broadcasted_iota(jnp.int32, (half, half), 0)
    return jnp.where(natural == theta_row, 1.0, 0.0).astype(BF16)


def pack_kernel(spectra_ref, out_ref):
    pairs = spectra_ref.shape[0]
    lane = lax.broadcasted_iota(jnp.int32, (2, LANES), 1)
    for i in range(pairs):
        for j in range(TILES - 1):
            out_ref[i * TILES + j] = spectra_ref[i, :, j * LANES : (j + 1) * LANES].astype(BF16)
        last = jnp.broadcast_to(spectra_ref[i, :, FULL:PACK], (2, LANES))
        out_ref[i * TILES + TILES - 1] = jnp.where(lane == 0, last, 0.0).astype(BF16)
    for t in range(pairs * TILES, out_ref.shape[0]):
        out_ref[t] = jnp.zeros((2, LANES), BF16)


def unpack_kernel(tiles_ref, out_ref):
    for i in range(out_ref.shape[0]):
        for j in range(TILES - 1):
            out_ref[i, :, j * LANES : (j + 1) * LANES] = tiles_ref[i * TILES + j].astype(F32)
        out_ref[i, :, FULL:PACK] = tiles_ref[i * TILES + TILES - 1].astype(F32)[:, 0:1]


def slot_masks(pair, column, order_odd):
    used = pair < NPAIRS
    low = jnp.where(used & (column <= LMAX - pair), 1.0, 0.0)
    high = jnp.where(used & (column > LMAX - pair), 1.0, 0.0)
    low_sign = (1 - 2 * (column & 1)).astype(F32)
    high_sign = (1 - 2 * ((column + pair) & 1)).astype(F32)
    return jnp.where(order_odd, high, low), jnp.where(order_odd, high_sign, low_sign)


def synthesis_kernel(
    pairs_ref, where_ref, source_ref, tiles_ref, theta_ref, out_ref, table_ref, rows_ref, arrived
):
    slots = table_ref.shape[0]
    copies = [
        pltpu.make_async_copy(source_ref.at[slot], table_ref.at[slot], arrived.at[slot])
        for slot in range(slots)
    ]
    for copy in copies:
        copy.start()
    owners = out_ref.shape[0]
    own_half = theta_ref.shape[1] // owners
    groups = rows_ref.shape[0]
    block = 6 * slots
    row = lax.broadcasted_iota(jnp.int32, (8, LANES), 0)
    odd = (row & 1) == 1
    field = row >> 1
    lane = lax.broadcasted_iota(jnp.int32, (8, LANES), 1)

    for slot in range(slots):
        if (slot - 2) % GROUP == 0 or slot == 0:
            for copy in copies[slot : slot + GROUP if slot else 2]:
                copy.wait()
        pair = pairs_ref[where_ref[0] * slots + slot]
        weight = jnp.where((pair == 0) & (row & 1 == 0), 1.0, 2.0)
        blocks = [[], [], [], []]
        for j in range(TILES):
            tiles = [tiles_ref[(f * slots + slot) * TILES + j].astype(F32) for f in range(3)]
            mask, sign = slot_masks(pair, lane + j * LANES, odd)
            mask = mask * weight
            for c in range(2):
                parts = [jnp.broadcast_to(t[c : c + 1], (8, LANES)) for t in tiles]
                base = jnp.where(field == 0, parts[0], jnp.where(field == 1, parts[1], parts[2]))
                base = base * mask
                blocks[2 * c].append(base)
                blocks[2 * c + 1].append(base * sign)
        left = jnp.concatenate([jnp.concatenate(b, axis=1) for b in blocks], axis=0)
        sums = jnp.dot(
            left[:, :FULL].astype(BF16), table_ref[slot, :FULL, :], preferred_element_type=F32
        )
        sums = sums + left[:, FULL : FULL + 1] * table_ref[slot, FULL:PACK, :].astype(F32)
        for k in range(4):
            for g in range(groups):
                rows_ref[g, pl.ds(k * block + slot, 6, stride=slots), :] = sums[
                    k * 8 : k * 8 + 6, g * LANES : (g + 1) * LANES
                ]
    select = one_hot(theta_ref[...])
    moved = []
    for k in range(4):
        rows = jnp.concatenate(
            [rows_ref[g, k * block : (k + 1) * block, :] for g in range(groups)], axis=1
        ).astype(BF16)
        moved.append(jnp.dot(rows, select, preferred_element_type=F32))
    for d in range(owners):
        out_ref[d] = jnp.concatenate(
            [m[:, d * own_half : (d + 1) * own_half] for m in moved], axis=1
        ).astype(BF16)


def table_kernel(coarse_cos_ref, coarse_sin_ref, fine_cos_ref, fine_sin_ref, out_ref):
    rows = fine_cos_ref.shape[0]
    fine_cos = fine_cos_ref[...]
    fine_sin = fine_sin_ref[...]
    for a in range(NPHI // LANES):
        cos_a = coarse_cos_ref[:, a : a + 1]
        sin_a = coarse_sin_ref[:, a : a + 1]
        span = slice(a * LANES, (a + 1) * LANES)
        out_ref[:rows, span] = (cos_a * fine_cos - sin_a * fine_sin).astype(BF16)
        out_ref[rows:, span] = (-(sin_a * fine_cos + cos_a * fine_sin)).astype(BF16)


def fourier_kernel(rows_ref, table_ref, flux_ref, out_ref, left_ref, both_ref, sum_ref):
    owners = rows_ref.shape[0]
    part = rows_ref.shape[1] // 3
    theta = rows_ref.shape[2] // 2
    orders = owners * part
    wide = [rows_ref[d].astype(F32) for d in range(owners)]
    for f in range(3):
        turned = jnp.concatenate([w[f * part : (f + 1) * part] for w in wide], axis=0).T
        left_ref[f * theta : (f + 1) * theta, :] = jnp.concatenate(
            [turned[:theta], turned[theta:]], axis=1
        ).astype(BF16)
    for q in range(NPHI // WIDTH):
        span = slice(q * WIDTH, (q + 1) * WIDTH)
        grid = jnp.dot(left_ref[...], table_ref[:, span], preferred_element_type=F32)
        for g in range(2):
            flux = (grid[:theta] * grid[(1 + g) * theta : (2 + g) * theta]).astype(BF16)
            flux_ref[g, :, span] = flux
            both_ref[g * theta : (g + 1) * theta, span] = flux
    sum_ref[...] = lax.dot_general(
        table_ref[...], both_ref[...], NT, preferred_element_type=F32
    ) * NPHI ** (-0.5)
    for d in range(owners):
        out_ref[d] = jnp.concatenate(
            [sum_ref[c * orders + d * part : c * orders + (d + 1) * part, :] for c in range(2)],
            axis=0,
        ).astype(BF16)


def analysis_kernel(pairs_ref, where_ref, rows_ref, table_ref, theta_ref, out_ref, nat_ref):
    slots = table_ref.shape[0]
    owners = rows_ref.shape[0]
    own_half = theta_ref.shape[1] // owners
    block = rows_ref.shape[1]
    groups = nat_ref.shape[0]
    select = one_hot(theta_ref[...])
    wide = [rows_ref[d].astype(F32) for d in range(owners)]
    for k in range(4):
        own = jnp.concatenate([w[:, k * own_half : (k + 1) * own_half] for w in wide], axis=1)
        nat = lax.dot_general(own.astype(BF16), select, NT, preferred_element_type=F32)
        for g in range(groups):
            nat_ref[g, k * block : (k + 1) * block, :] = nat[:, g * LANES : (g + 1) * LANES]
    for t in range(2 * slots * TILES, out_ref.shape[0]):
        out_ref[t] = jnp.zeros((2, LANES), BF16)
    row = lax.broadcasted_iota(jnp.int32, (16, LANES), 0)
    odd = (row & 1) == 1
    south = (row & 4) == 4
    lane = lax.broadcasted_iota(jnp.int32, (16, LANES), 1)

    for slot in range(slots):
        left = jnp.concatenate(
            [nat_ref[g, pl.ds(slot, 16, stride=slots), :] for g in range(groups)], axis=1
        )
        sums = lax.dot_general(
            left.astype(BF16), table_ref[slot, :FULL, :], NT, preferred_element_type=F32
        )
        last = jnp.sum(left * table_ref[slot, FULL:PACK, :].astype(F32), axis=1, keepdims=True)
        pair = pairs_ref[where_ref[0] * slots + slot]
        for j in range(TILES):
            mask, sign = slot_masks(pair, lane + j * LANES, odd)
            if j < TILES - 1:
                part = sums[:, j * LANES : (j + 1) * LANES]
            else:
                part = jnp.where(lane == 0, last, 0.0)
            part = part * mask * jnp.where(south, sign, 1.0)
            for g in range(2):
                both = part[g * 8 : g * 8 + 4] + part[g * 8 + 4 : g * 8 + 8]
                tile = jnp.concatenate([both[0:1] + both[1:2], both[2:3] + both[3:4]], axis=0)
                out_ref[(g * slots + slot) * TILES + j] = tile.astype(BF16)


def call(kernel, name, out_shape, operands, scratch=(), scalars=0):
    operands = [
        x if i < scalars else pltpu.with_memory_space_constraint(x, pltpu.VMEM)
        for i, x in enumerate(operands)
    ]
    return pl.pallas_call(
        kernel,
        out_shape=tuple(pltpu.VMEM(shape, dtype) for shape, dtype in out_shape),
        in_specs=[
            pl.BlockSpec(memory_space=pltpu.SMEM if i < scalars else pltpu.VMEM)
            for i in range(len(operands))
        ],
        out_specs=(pl.BlockSpec(memory_space=pltpu.VMEM),) * len(out_shape),
        scratch_shapes=scratch,
        compiler_params=pltpu.CompilerParams(vmem_limit_bytes=SCOPED),
        name=name,
    )(*operands)


def level_mix(tiles, matrix, beside=None):
    levels = matrix.shape[0]
    share = tiles.shape[0] // levels
    here = lax.all_to_all(tiles, "row", split_axis=0, concat_axis=0, tiled=True)
    here, beside = lax.optimization_barrier((here, beside))
    here = here.reshape(levels, share * 2 * LANES).astype(F32)
    mixed = jnp.dot(matrix, here, precision=HIGH).astype(BF16)
    mixed = mixed.reshape(levels * share, 2, LANES)
    return lax.all_to_all(mixed, "row", split_axis=0, concat_axis=0, tiled=True), beside


def trig_table(pair_slots, owners, slot_dev):
    pairs = pair_slots.reshape(owners, 1, slot_dev)
    orders = jnp.concatenate([pairs, LMAX - pairs], axis=1).reshape(-1, 1)
    span = lax.broadcasted_iota(jnp.int32, (1, LANES), 1)
    coarse = (orders * (span * LANES)) % NPHI
    fine = (orders * span) % NPHI
    scale = 2.0 * math.pi / NPHI
    coarse = coarse.astype(F32) * scale
    fine = fine.astype(F32) * scale
    shape = (2 * orders.shape[0], NPHI)
    trig = (jnp.cos(coarse), jnp.sin(coarse), jnp.cos(fine), jnp.sin(fine))
    return call(table_kernel, "table", [(shape, BF16)], trig)[0]


def local(spectra, legendre, pair_slots, theta_owner):
    slot_dev, _, half = legendre.shape
    owners = lax.axis_size("ma")
    levels = lax.axis_size("row") * spectra.shape[0]
    theta_dev = 2 * half // owners
    groups = half // LANES
    synth_mat, analysis_mat = chebyshev_pair(levels)
    where = lax.axis_index("ma").astype(jnp.int32).reshape(1)
    theta_row = theta_owner.reshape(1, half)
    table = trig_table(pair_slots, owners, slot_dev)

    flat = jnp.transpose(spectra, (0, 1, 2, 4, 3)).reshape(3 * slot_dev, 2, PACK)
    share = -(-3 * slot_dev * TILES // levels)
    (tiles,) = pl.pallas_call(
        pack_kernel,
        out_shape=(pltpu.VMEM((share * levels, 2, LANES), BF16),),
        out_specs=(pl.BlockSpec(memory_space=pltpu.VMEM),),
        compiler_params=pltpu.CompilerParams(vmem_limit_bytes=SCOPED),
        name="pack",
    )(flat)
    tiles, (table, theta_row, where) = level_mix(tiles, synth_mat, (table, theta_row, where))

    vmem = pl.BlockSpec(memory_space=pltpu.VMEM)
    smem = pl.BlockSpec(memory_space=pltpu.SMEM)
    outgoing, legendre = pl.pallas_call(
        synthesis_kernel,
        out_shape=(
            pltpu.VMEM((owners, 6 * slot_dev, LANES), BF16),
            pltpu.VMEM(legendre.shape, BF16),
        ),
        in_specs=[smem, smem, pl.BlockSpec(memory_space=pltpu.HBM), vmem, vmem],
        out_specs=(vmem, vmem),
        scratch_shapes=[
            pltpu.VMEM((groups, 24 * slot_dev, LANES), F32),
            pltpu.SemaphoreType.DMA((slot_dev,)),
        ],
        compiler_params=pltpu.CompilerParams(vmem_limit_bytes=SYNTHESIS_SCOPED),
        name="synthesis",
    )(
        pair_slots,
        where,
        legendre,
        pltpu.with_memory_space_constraint(tiles, pltpu.VMEM),
        pltpu.with_memory_space_constraint(theta_row, pltpu.VMEM),
    )
    rows = lax.all_to_all(outgoing, "ma", split_axis=0, concat_axis=0, tiled=True)

    orders = table.shape[0]
    flux, fourier = call(
        fourier_kernel,
        "fourier",
        [((2, theta_dev, NPHI), BF16), ((owners, 4 * slot_dev, 2 * theta_dev), BF16)],
        (rows, table),
        [
            pltpu.VMEM((3 * theta_dev, orders), BF16),
            pltpu.VMEM((2 * theta_dev, NPHI), BF16),
            pltpu.VMEM((orders, 2 * theta_dev), F32),
        ],
    )
    returned = lax.all_to_all(fourier, "ma", split_axis=0, concat_axis=0, tiled=True)

    share = -(-2 * slot_dev * TILES // levels)
    (tiles,) = call(
        analysis_kernel,
        "analysis",
        [((share * levels, 2, LANES), BF16)],
        (pair_slots, where, returned, legendre, theta_row),
        [pltpu.VMEM((groups, 16 * slot_dev, LANES), F32)],
        scalars=2,
    )
    flux = jnp.transpose(flux, (1, 0, 2))[None]
    tiles, flux = level_mix(tiles, analysis_mat, flux)
    tiles = pltpu.with_memory_space_constraint(tiles, pltpu.VMEM)
    result = pl.pallas_call(
        unpack_kernel,
        out_shape=jax.ShapeDtypeStruct((2 * slot_dev, 2, PACK), F32),
        in_specs=[pl.BlockSpec(memory_space=pltpu.VMEM)],
        compiler_params=pltpu.CompilerParams(vmem_limit_bytes=SCOPED),
        name="unpack",
    )(tiles)
    result = jnp.transpose(result.reshape(1, 2, slot_dev, 2, PACK), (0, 1, 2, 4, 3))
    return flux, result


def solution(mesh):
    in_specs = (P("row", None, "ma", None, None), P("ma", None, None), P(), P())
    out_specs = (P("row", "ma", None, None), P("row", None, "ma", None, None))
    return jax.shard_map(local, mesh=mesh, in_specs=in_specs, out_specs=out_specs, check_vma=False)
```

```python
import math

import jax
import jax.numpy as jnp
import numpy as np
from jax import lax
from jax.experimental import pallas as pl
from jax.experimental.pallas import tpu as pltpu
from jax.sharding import PartitionSpec as P

LMAX = 511
NPHI = 1536
NPAIRS = 256
PACK = 513
LANES = 128
TILES = -(-PACK // LANES)
FULL = PACK // LANES * LANES
WIDTH = 256
SCOPED = 16 << 20
SYNTHESIS_SCOPED = 46 << 20
GROUP = 4
BF16 = jnp.bfloat16
F32 = jnp.float32
NT = (((1,), (1,)), ((), ()))


def chebyshev_pair(levels):
    index = np.arange(levels)
    cosines = np.cos(np.pi * (np.outer(index, index) % (2 * (levels - 1))) / (levels - 1))
    ends = np.where((index == 0) | (index == levels - 1), 0.5, 1.0)
    analysis = (2.0 / (levels - 1)) ** 0.5 * np.outer(ends, ends) * cosines
    return cosines.astype(np.float32), analysis.astype(np.float32)


def one_hot(theta_row):
    half = theta_row.shape[1]
    natural = lax.broadcasted_iota(jnp.int32, (half, half), 0)
    return jnp.where(natural == theta_row, 1.0, 0.0).astype(BF16)


def pack_kernel(spectra_ref, out_ref):
    pairs = spectra_ref.shape[0]
    whole = PACK // LANES
    lane = lax.broadcasted_iota(jnp.int32, (2, LANES), 1)
    last = jnp.zeros((2, LANES), F32)
    for i in range(pairs):
        for j in range(whole):
            out_ref[i * whole + j] = spectra_ref[i, :, j * LANES : (j + 1) * LANES].astype(BF16)
        value = jnp.broadcast_to(spectra_ref[i, :, FULL:PACK], (2, LANES))
        last = jnp.where(lane == i, value, last)
    out_ref[pairs * whole] = last.astype(BF16)
    for t in range(pairs * whole + 1, out_ref.shape[0]):
        out_ref[t] = jnp.zeros((2, LANES), BF16)


def unpack_kernel(tiles_ref, out_ref):
    for i in range(out_ref.shape[0]):
        for j in range(TILES - 1):
            out_ref[i, :, j * LANES : (j + 1) * LANES] = tiles_ref[i * TILES + j].astype(F32)
        out_ref[i, :, FULL:PACK] = tiles_ref[i * TILES + TILES - 1].astype(F32)[:, 0:1]


def slot_masks(pair, column, order_odd):
    used = pair < NPAIRS
    low = jnp.where(used & (column <= LMAX - pair), 1.0, 0.0)
    high = jnp.where(used & (column > LMAX - pair), 1.0, 0.0)
    low_sign = (1 - 2 * (column & 1)).astype(F32)
    high_sign = (1 - 2 * ((column + pair) & 1)).astype(F32)
    return jnp.where(order_odd, high, low), jnp.where(order_odd, high_sign, low_sign)


def synthesis_kernel(
    pairs_ref, where_ref, source_ref, tiles_ref, theta_ref, out_ref, table_ref, rows_ref, arrived
):
    slots = table_ref.shape[0]
    copies = [
        pltpu.make_async_copy(source_ref.at[slot], table_ref.at[slot], arrived.at[slot])
        for slot in range(slots)
    ]
    for copy in copies:
        copy.start()
    owners = out_ref.shape[0]
    own_half = theta_ref.shape[1] // owners
    groups = rows_ref.shape[0]
    block = 6 * slots
    row = lax.broadcasted_iota(jnp.int32, (8, LANES), 0)
    odd = (row & 1) == 1
    field = row >> 1
    lane = lax.broadcasted_iota(jnp.int32, (8, LANES), 1)
    last = tiles_ref[3 * slots * (TILES - 1)].astype(F32)

    for slot in range(slots):
        if (slot - 2) % GROUP == 0 or slot == 0:
            for copy in copies[slot : slot + GROUP if slot else 2]:
                copy.wait()
        pair = pairs_ref[where_ref[0] * slots + slot]
        weight = jnp.where((pair == 0) & (row & 1 == 0), 1.0, 2.0)
        blocks = [[], [], [], []]
        for j in range(TILES):
            if j < TILES - 1:
                tiles = [
                    tiles_ref[(f * slots + slot) * (TILES - 1) + j].astype(F32) for f in range(3)
                ]
            else:
                tiles = [
                    jnp.broadcast_to(last[:, f * slots + slot : f * slots + slot + 1], (2, LANES))
                    for f in range(3)
                ]
            mask, sign = slot_masks(pair, lane + j * LANES, odd)
            mask = mask * weight
            for c in range(2):
                parts = [jnp.broadcast_to(t[c : c + 1], (8, LANES)) for t in tiles]
                base = jnp.where(field == 0, parts[0], jnp.where(field == 1, parts[1], parts[2]))
                base = base * mask
                blocks[2 * c].append(base)
                blocks[2 * c + 1].append(base * sign)
        left = jnp.concatenate([jnp.concatenate(b, axis=1) for b in blocks], axis=0)
        sums = jnp.dot(
            left[:, :FULL].astype(BF16), table_ref[slot, :FULL, :], preferred_element_type=F32
        )
        sums = sums + left[:, FULL : FULL + 1] * table_ref[slot, FULL:PACK, :].astype(F32)
        for k in range(4):
            for g in range(groups):
                rows_ref[g, pl.ds(k * block + slot, 6, stride=slots), :] = sums[
                    k * 8 : k * 8 + 6, g * LANES : (g + 1) * LANES
                ]
    select = one_hot(theta_ref[...])
    moved = []
    for k in range(4):
        rows = jnp.concatenate(
            [rows_ref[g, k * block : (k + 1) * block, :] for g in range(groups)], axis=1
        ).astype(BF16)
        moved.append(jnp.dot(rows, select, preferred_element_type=F32))
    for d in range(owners):
        out_ref[d] = jnp.concatenate(
            [m[:, d * own_half : (d + 1) * own_half] for m in moved], axis=1
        ).astype(BF16)


def table_kernel(
    coarse_cos_ref, coarse_sin_ref, fine_cos_ref, fine_sin_ref, matrix_ref, out_ref, kept_ref
):
    kept_ref[...] = matrix_ref[...]
    rows = fine_cos_ref.shape[0]
    fine_cos = fine_cos_ref[...]
    fine_sin = fine_sin_ref[...]
    for a in range(NPHI // LANES):
        cos_a = coarse_cos_ref[:, a : a + 1]
        sin_a = coarse_sin_ref[:, a : a + 1]
        span = slice(a * LANES, (a + 1) * LANES)
        out_ref[:rows, span] = (cos_a * fine_cos - sin_a * fine_sin).astype(BF16)
        out_ref[rows:, span] = (-(sin_a * fine_cos + cos_a * fine_sin)).astype(BF16)


def fourier_kernel(rows_ref, table_ref, flux_ref, out_ref, left_ref, both_ref, sum_ref):
    owners = rows_ref.shape[0]
    part = rows_ref.shape[1] // 3
    theta = rows_ref.shape[2] // 2
    orders = owners * part
    wide = [rows_ref[d].astype(F32) for d in range(owners)]
    for f in range(3):
        turned = jnp.concatenate([w[f * part : (f + 1) * part] for w in wide], axis=0).T
        left_ref[f * theta : (f + 1) * theta, :] = jnp.concatenate(
            [turned[:theta], turned[theta:]], axis=1
        ).astype(BF16)
    for q in range(NPHI // WIDTH):
        span = slice(q * WIDTH, (q + 1) * WIDTH)
        grid = jnp.dot(left_ref[...], table_ref[:, span], preferred_element_type=F32)
        for g in range(2):
            flux = (grid[:theta] * grid[(1 + g) * theta : (2 + g) * theta]).astype(BF16)
            flux_ref[g, :, span] = flux
            both_ref[g * theta : (g + 1) * theta, span] = flux
    sum_ref[...] = lax.dot_general(
        table_ref[...], both_ref[...], NT, preferred_element_type=F32
    ) * NPHI ** (-0.5)
    for d in range(owners):
        out_ref[d] = jnp.concatenate(
            [sum_ref[c * orders + d * part : c * orders + (d + 1) * part, :] for c in range(2)],
            axis=0,
        ).astype(BF16)


def analysis_kernel(pairs_ref, where_ref, rows_ref, table_ref, theta_ref, out_ref, nat_ref):
    slots = table_ref.shape[0]
    owners = rows_ref.shape[0]
    own_half = theta_ref.shape[1] // owners
    block = rows_ref.shape[1]
    groups = nat_ref.shape[0]
    select = one_hot(theta_ref[...])
    wide = [rows_ref[d].astype(F32) for d in range(owners)]
    for k in range(4):
        own = jnp.concatenate([w[:, k * own_half : (k + 1) * own_half] for w in wide], axis=1)
        nat = lax.dot_general(own.astype(BF16), select, NT, preferred_element_type=F32)
        for g in range(groups):
            nat_ref[g, k * block : (k + 1) * block, :] = nat[:, g * LANES : (g + 1) * LANES]
    for t in range(2 * slots * TILES, out_ref.shape[0]):
        out_ref[t] = jnp.zeros((2, LANES), BF16)
    row = lax.broadcasted_iota(jnp.int32, (16, LANES), 0)
    odd = (row & 1) == 1
    south = (row & 4) == 4
    lane = lax.broadcasted_iota(jnp.int32, (16, LANES), 1)

    for slot in range(slots):
        left = jnp.concatenate(
            [nat_ref[g, pl.ds(slot, 16, stride=slots), :] for g in range(groups)], axis=1
        )
        sums = lax.dot_general(
            left.astype(BF16), table_ref[slot, :FULL, :], NT, preferred_element_type=F32
        )
        last = jnp.sum(left * table_ref[slot, FULL:PACK, :].astype(F32), axis=1, keepdims=True)
        pair = pairs_ref[where_ref[0] * slots + slot]
        for j in range(TILES):
            mask, sign = slot_masks(pair, lane + j * LANES, odd)
            if j < TILES - 1:
                part = sums[:, j * LANES : (j + 1) * LANES]
            else:
                part = jnp.where(lane == 0, last, 0.0)
            part = part * mask * jnp.where(south, sign, 1.0)
            for g in range(2):
                both = part[g * 8 : g * 8 + 4] + part[g * 8 + 4 : g * 8 + 8]
                tile = jnp.concatenate([both[0:1] + both[1:2], both[2:3] + both[3:4]], axis=0)
                out_ref[(g * slots + slot) * TILES + j] = tile.astype(BF16)


def call(kernel, name, out_shape, operands, scratch=(), scalars=0):
    operands = [
        x if i < scalars else pltpu.with_memory_space_constraint(x, pltpu.VMEM)
        for i, x in enumerate(operands)
    ]
    return pl.pallas_call(
        kernel,
        out_shape=tuple(pltpu.VMEM(shape, dtype) for shape, dtype in out_shape),
        in_specs=[
            pl.BlockSpec(memory_space=pltpu.SMEM if i < scalars else pltpu.VMEM)
            for i in range(len(operands))
        ],
        out_specs=(pl.BlockSpec(memory_space=pltpu.VMEM),) * len(out_shape),
        scratch_shapes=scratch,
        compiler_params=pltpu.CompilerParams(vmem_limit_bytes=SCOPED),
        name=name,
    )(*operands)


def mix_kernel(tiles_ref, matrix_ref, out_ref, wide_ref):
    levels = matrix_ref.shape[0]
    count = tiles_ref.shape[0]
    rows = 2 * count // levels
    for t in range(count):
        wide_ref[2 * t : 2 * t + 2, :] = tiles_ref[t].astype(F32)
    right = jnp.concatenate(
        [wide_ref[pl.ds(i, levels, stride=rows), :] for i in range(rows)], axis=1
    ).astype(BF16)
    right = jnp.concatenate([right, right], axis=0)
    mixed = jnp.dot(matrix_ref[...], right, preferred_element_type=F32)
    for i in range(rows):
        wide_ref[pl.ds(i, levels, stride=rows), :] = mixed[:, i * LANES : (i + 1) * LANES]
    for t in range(count):
        out_ref[t] = wide_ref[2 * t : 2 * t + 2, :].astype(BF16)


def two_parts(matrix):
    upper = jnp.asarray(matrix).astype(BF16)
    lower = (matrix - upper.astype(F32)).astype(BF16)
    return jnp.concatenate([upper, lower], axis=1)


def level_mix(tiles, parts, beside=None):
    here = lax.all_to_all(tiles, "row", split_axis=0, concat_axis=0, tiled=True)
    here, beside, parts = lax.optimization_barrier((here, beside, parts))
    (mixed,) = call(
        mix_kernel,
        "mix",
        [(tiles.shape, BF16)],
        (here, parts),
        [pltpu.VMEM((2 * tiles.shape[0], LANES), F32)],
    )
    return lax.all_to_all(mixed, "row", split_axis=0, concat_axis=0, tiled=True), beside


def trig_table(pair_slots, owners, slot_dev, parts):
    pairs = pair_slots.reshape(owners, 1, slot_dev)
    orders = jnp.concatenate([pairs, LMAX - pairs], axis=1).reshape(-1, 1)
    span = lax.broadcasted_iota(jnp.int32, (1, LANES), 1)
    coarse = (orders * (span * LANES)) % NPHI
    fine = (orders * span) % NPHI
    scale = 2.0 * math.pi / NPHI
    coarse = coarse.astype(F32) * scale
    fine = fine.astype(F32) * scale
    shape = (2 * orders.shape[0], NPHI)
    trig = (jnp.cos(coarse), jnp.sin(coarse), jnp.cos(fine), jnp.sin(fine))
    return call(table_kernel, "table", [(shape, BF16), (parts.shape, BF16)], trig + (parts,))


def local(spectra, legendre, pair_slots, theta_owner):
    slot_dev, _, half = legendre.shape
    owners = lax.axis_size("ma")
    levels = lax.axis_size("row") * spectra.shape[0]
    theta_dev = 2 * half // owners
    groups = half // LANES
    synth_mat, analysis_mat = chebyshev_pair(levels)
    where = lax.axis_index("ma").astype(jnp.int32).reshape(1)
    theta_row = theta_owner.reshape(1, half)
    table, synth_parts = trig_table(pair_slots, owners, slot_dev, two_parts(synth_mat))

    flat = jnp.transpose(spectra, (0, 1, 2, 4, 3)).reshape(3 * slot_dev, 2, PACK)
    share = -(-(3 * slot_dev * (TILES - 1) + 1) // levels)
    (tiles,) = pl.pallas_call(
        pack_kernel,
        out_shape=(pltpu.VMEM((share * levels, 2, LANES), BF16),),
        out_specs=(pl.BlockSpec(memory_space=pltpu.VMEM),),
        compiler_params=pltpu.CompilerParams(vmem_limit_bytes=SCOPED),
        name="pack",
    )(flat)
    tiles, (table, theta_row, where) = level_mix(tiles, synth_parts, (table, theta_row, where))

    vmem = pl.BlockSpec(memory_space=pltpu.VMEM)
    smem = pl.BlockSpec(memory_space=pltpu.SMEM)
    outgoing, legendre = pl.pallas_call(
        synthesis_kernel,
        out_shape=(
            pltpu.VMEM((owners, 6 * slot_dev, LANES), BF16),
            pltpu.VMEM(legendre.shape, BF16),
        ),
        in_specs=[smem, smem, pl.BlockSpec(memory_space=pltpu.HBM), vmem, vmem],
        out_specs=(vmem, vmem),
        scratch_shapes=[
            pltpu.VMEM((groups, 24 * slot_dev, LANES), F32),
            pltpu.SemaphoreType.DMA((slot_dev,)),
        ],
        compiler_params=pltpu.CompilerParams(vmem_limit_bytes=SYNTHESIS_SCOPED),
        name="synthesis",
    )(
        pair_slots,
        where,
        legendre,
        pltpu.with_memory_space_constraint(tiles, pltpu.VMEM),
        pltpu.with_memory_space_constraint(theta_row, pltpu.VMEM),
    )
    rows = lax.all_to_all(outgoing, "ma", split_axis=0, concat_axis=0, tiled=True)

    orders = table.shape[0]
    flux, fourier = call(
        fourier_kernel,
        "fourier",
        [((2, theta_dev, NPHI), BF16), ((owners, 4 * slot_dev, 2 * theta_dev), BF16)],
        (rows, table),
        [
            pltpu.VMEM((3 * theta_dev, orders), BF16),
            pltpu.VMEM((2 * theta_dev, NPHI), BF16),
            pltpu.VMEM((orders, 2 * theta_dev), F32),
        ],
    )
    returned = lax.all_to_all(fourier, "ma", split_axis=0, concat_axis=0, tiled=True)

    share = -(-2 * slot_dev * TILES // levels)
    (tiles,) = call(
        analysis_kernel,
        "analysis",
        [((share * levels, 2, LANES), BF16)],
        (pair_slots, where, returned, legendre, theta_row),
        [pltpu.VMEM((groups, 16 * slot_dev, LANES), F32)],
        scalars=2,
    )
    flux = jnp.transpose(flux, (1, 0, 2))[None]
    tiles, flux = level_mix(tiles, two_parts(analysis_mat), flux)
    tiles = pltpu.with_memory_space_constraint(tiles, pltpu.VMEM)
    result = pl.pallas_call(
        unpack_kernel,
        out_shape=jax.ShapeDtypeStruct((2 * slot_dev, 2, PACK), F32),
        in_specs=[pl.BlockSpec(memory_space=pltpu.VMEM)],
        compiler_params=pltpu.CompilerParams(vmem_limit_bytes=SCOPED),
        name="unpack",
    )(tiles)
    result = jnp.transpose(result.reshape(1, 2, slot_dev, 2, PACK), (0, 1, 2, 4, 3))
    return flux, result


def solution(mesh):
    in_specs = (P("row", None, "ma", None, None), P("ma", None, None), P(), P())
    out_specs = (P("row", "ma", None, None), P("row", None, "ma", None, None))
    return jax.shard_map(local, mesh=mesh, in_specs=in_specs, out_specs=out_specs, check_vma=False)
```

```python
import math

import jax
import jax.numpy as jnp
import numpy as np
from jax import lax
from jax.experimental import pallas as pl
from jax.experimental.pallas import tpu as pltpu
from jax.sharding import PartitionSpec as P

LMAX = 511
NPHI = 1536
NPAIRS = 256
PACK = 513
LANES = 128
TILES = -(-PACK // LANES)
FULL = PACK // LANES * LANES
WIDTH = 256
SCOPED = 16 << 20
LEGENDRE_SCOPED = 56 << 20
GROUP = 4
BF16 = jnp.bfloat16
F32 = jnp.float32
NT = (((1,), (1,)), ((), ()))


def chebyshev_pair(levels):
    index = np.arange(levels)
    cosines = np.cos(np.pi * (np.outer(index, index) % (2 * (levels - 1))) / (levels - 1))
    ends = np.where((index == 0) | (index == levels - 1), 0.5, 1.0)
    analysis = (2.0 / (levels - 1)) ** 0.5 * np.outer(ends, ends) * cosines
    return cosines.astype(np.float32), analysis.astype(np.float32)


def one_hot(theta_row):
    half = theta_row.shape[1]
    natural = lax.broadcasted_iota(jnp.int32, (half, half), 0)
    return jnp.where(natural == theta_row, 1.0, 0.0).astype(BF16)


def slot_masks(pair, column, order_odd):
    used = pair < NPAIRS
    low = jnp.where(used & (column <= LMAX - pair), 1.0, 0.0)
    high = jnp.where(used & (column > LMAX - pair), 1.0, 0.0)
    low_sign = (1 - 2 * (column & 1)).astype(F32)
    high_sign = (1 - 2 * ((column + pair) & 1)).astype(F32)
    return jnp.where(order_odd, high, low), jnp.where(order_odd, high_sign, low_sign)


def start_copies(source_ref, table_ref, arrived):
    copies = [
        pltpu.make_async_copy(source_ref.at[slot], table_ref.at[slot], arrived.at[slot])
        for slot in range(table_ref.shape[0])
    ]
    for copy in copies:
        copy.start()
    return copies


def wait_group(copies, slot):
    if slot == 0 or (slot - 2) % GROUP == 0:
        for copy in copies[slot : slot + GROUP if slot else 2]:
            copy.wait()


def synthesis_kernel(
    pairs_ref, source_ref, spectra_ref, theta_ref, out_ref, rows_ref, table_ref, arrived
):
    slots = table_ref.shape[0]
    copies = start_copies(source_ref, table_ref, arrived)
    first = lax.axis_index("ma") * slots
    owners = out_ref.shape[0]
    own_half = theta_ref.shape[1] // owners
    groups = rows_ref.shape[0]
    block = 6 * slots
    row = lax.broadcasted_iota(jnp.int32, (8, LANES), 0)
    odd = (row & 1) == 1
    field = row >> 1
    lane = lax.broadcasted_iota(jnp.int32, (8, LANES), 1)

    for slot in range(slots):
        wait_group(copies, slot)
        pair = pairs_ref[first + slot]
        weight = jnp.where((pair == 0) & (row & 1 == 0), 1.0, 2.0)
        blocks = [[], [], [], []]
        for j in range(TILES):
            picked = [f * slots + slot for f in range(3)]
            if j < TILES - 1:
                tiles = [spectra_ref[i, :, j * LANES : (j + 1) * LANES] for i in picked]
            else:
                tiles = [
                    jnp.broadcast_to(spectra_ref[i, :, FULL:PACK], (2, LANES)) for i in picked
                ]
            mask, sign = slot_masks(pair, lane + j * LANES, odd)
            mask = mask * weight
            for c in range(2):
                parts = [jnp.broadcast_to(t[c : c + 1], (8, LANES)) for t in tiles]
                base = jnp.where(field == 0, parts[0], jnp.where(field == 1, parts[1], parts[2]))
                base = base * mask
                blocks[2 * c].append(base)
                blocks[2 * c + 1].append(base * sign)
        left = jnp.concatenate([jnp.concatenate(b, axis=1) for b in blocks], axis=0)
        sums = jnp.dot(
            left[:, :FULL].astype(BF16), table_ref[slot, :FULL, :], preferred_element_type=F32
        )
        sums = sums + left[:, FULL : FULL + 1] * table_ref[slot, FULL:PACK, :].astype(F32)
        for k in range(4):
            for g in range(groups):
                rows_ref[g, pl.ds(k * block + slot, 6, stride=slots), :] = sums[
                    k * 8 : k * 8 + 6, g * LANES : (g + 1) * LANES
                ]
    select = one_hot(theta_ref[...])
    moved = []
    for k in range(4):
        rows = jnp.concatenate(
            [rows_ref[g, k * block : (k + 1) * block, :] for g in range(groups)], axis=1
        ).astype(BF16)
        moved.append(jnp.dot(rows, select, preferred_element_type=F32))
    for d in range(owners):
        out_ref[d] = jnp.concatenate(
            [m[:, d * own_half : (d + 1) * own_half] for m in moved], axis=1
        ).astype(BF16)


def table_kernel(
    coarse_cos_ref, coarse_sin_ref, fine_cos_ref, fine_sin_ref, synth_ref, analysis_ref,
    out_ref, kept_synth_ref, kept_analysis_ref,
):
    kept_synth_ref[...] = synth_ref[...]
    kept_analysis_ref[...] = analysis_ref[...]
    rows = fine_cos_ref.shape[0]
    fine_cos = fine_cos_ref[...]
    fine_sin = fine_sin_ref[...]
    for a in range(NPHI // LANES):
        cos_a = coarse_cos_ref[:, a : a + 1]
        sin_a = coarse_sin_ref[:, a : a + 1]
        span = slice(a * LANES, (a + 1) * LANES)
        out_ref[:rows, span] = (cos_a * fine_cos - sin_a * fine_sin).astype(BF16)
        out_ref[rows:, span] = (-(sin_a * fine_cos + cos_a * fine_sin)).astype(BF16)


def scatter_row(wide_ref, row, rows, value):
    wide_ref[pl.ds(row, value.shape[0], stride=rows), :] = value


def scatter_rows(wide_ref, row, rows, values):
    full = values[0].shape[1] // LANES
    for value in values:
        for j in range(full):
            scatter_row(wide_ref, row, rows, value[:, j * LANES : (j + 1) * LANES])
            row += 1
    rest = [value[:, full * LANES :] for value in values]
    filled = sum(r.shape[1] for r in rest)
    rest.append(jnp.zeros((rest[0].shape[0], LANES - filled), F32))
    scatter_row(wide_ref, row, rows, jnp.concatenate(rest, axis=1))
    scatter_row(wide_ref, row + 1, rows, jnp.zeros_like(values[0][:, :LANES]))


def gather_rows(wide_ref, count, rows, arrays, width):
    full = width // LANES
    line = lambda row: wide_ref[pl.ds(row, count, stride=rows), :]
    rest = line(arrays * full)
    part = width - full * LANES
    return [
        jnp.concatenate(
            [line(a * full + j) for j in range(full)] + [rest[:, a * part : (a + 1) * part]],
            axis=1,
        )
        for a in range(arrays)
    ]


def widen(tiles_ref, wide_ref, count, stride, taken):
    for i in range(count):
        for t in range(taken):
            line = 2 * (i * taken + t)
            wide_ref[line : line + 2, :] = tiles_ref[i * stride + t].astype(F32)


def narrow(wide_ref, tiles_ref):
    for t in range(tiles_ref.shape[0]):
        tiles_ref[t] = wide_ref[2 * t : 2 * t + 2, :].astype(BF16)


def turn_kernel(rows_ref, out_ref, wide_ref):
    owners = rows_ref.shape[0]
    part = rows_ref.shape[1] // 3
    theta = rows_ref.shape[2] // 2
    wide = [rows_ref[d].astype(F32) for d in range(owners)]
    lines = []
    for f in range(3):
        turned = jnp.concatenate([w[f * part : (f + 1) * part] for w in wide], axis=0).T
        lines.append(jnp.concatenate([turned[:theta], turned[theta:]], axis=1))
    scatter_rows(wide_ref, 0, wide_ref.shape[0] // theta, lines)
    narrow(wide_ref, out_ref)


def grid_kernel(
    tiles_ref, table_ref, synth_ref, analysis_ref, out_ref, wide_ref, left_ref, both_ref, out_wide_ref
):
    levels = synth_ref.shape[0]
    orders = table_ref.shape[0]
    per_level = tiles_ref.shape[0] // levels
    widen(tiles_ref, wide_ref, levels, per_level, per_level)
    for f, line in enumerate(gather_rows(wide_ref, levels, 2 * per_level, 3, orders)):
        line = line.astype(BF16)
        left_ref[f * levels : (f + 1) * levels, :] = jnp.dot(
            synth_ref[...], jnp.concatenate([line, line], axis=0), preferred_element_type=F32
        ).astype(BF16)
    rows = out_wide_ref.shape[0] // levels
    flux_row = rows - 2 * NPHI // LANES
    for q in range(NPHI // WIDTH):
        span = slice(q * WIDTH, (q + 1) * WIDTH)
        grid = jnp.dot(left_ref[...], table_ref[:, span], preferred_element_type=F32)
        for g in range(2):
            flux = (grid[:levels] * grid[(1 + g) * levels : (2 + g) * levels]).astype(BF16)
            both_ref[g * levels : (g + 1) * levels, span] = flux
            flux = flux.astype(F32)
            for j in range(WIDTH // LANES):
                row = flux_row + 2 * (q * (WIDTH // LANES) + j) + g
                scatter_row(out_wide_ref, row, rows, flux[:, j * LANES : (j + 1) * LANES])
    fourier = lax.dot_general(
        both_ref[...], table_ref[...], NT, preferred_element_type=F32
    ) * NPHI ** (-0.5)
    mixed = []
    for g in range(2):
        value = fourier[g * levels : (g + 1) * levels]
        upper = value.astype(BF16)
        lower = (value - upper.astype(F32)).astype(BF16)
        right = jnp.concatenate([upper, lower, upper], axis=0)
        mixed.append(jnp.dot(analysis_ref[...], right, preferred_element_type=F32))
    scatter_rows(out_wide_ref, 0, rows, mixed)
    narrow(out_wide_ref, out_ref)


def return_kernel(tiles_ref, out_ref, wide_ref, sum_ref):
    owners = out_ref.shape[0]
    part = out_ref.shape[1] // 2
    orders = 2 * owners * part
    theta = out_ref.shape[2] // 2
    taken = wide_ref.shape[0] // (2 * theta)
    widen(tiles_ref, wide_ref, theta, tiles_ref.shape[0] // theta, taken)
    lines = gather_rows(wide_ref, theta, 2 * taken, 2, orders)
    sum_ref[...] = jnp.concatenate(lines, axis=0).T
    for d in range(owners):
        out_ref[d] = jnp.concatenate(
            [
                sum_ref[c * owners * part + d * part : c * owners * part + (d + 1) * part, :]
                for c in range(2)
            ],
            axis=0,
        ).astype(BF16)


def flux_kernel(tiles_ref, out_ref):
    theta = out_ref.shape[0]
    stride = tiles_ref.shape[0] // theta
    count = NPHI // LANES
    for t in range(theta):
        for q in range(count):
            out_ref[t, :, q * LANES : (q + 1) * LANES] = tiles_ref[t * stride + stride - count + q]


def analysis_kernel(
    pairs_ref, source_ref, rows_ref, theta_ref, out_ref, nat_ref, table_ref, arrived
):
    slots = table_ref.shape[0]
    copies = start_copies(source_ref, table_ref, arrived)
    first = lax.axis_index("ma") * slots
    owners = rows_ref.shape[0]
    own_half = theta_ref.shape[1] // owners
    block = rows_ref.shape[1]
    groups = nat_ref.shape[0]
    select = one_hot(theta_ref[...])
    wide = [rows_ref[d].astype(F32) for d in range(owners)]
    for k in range(4):
        own = jnp.concatenate([w[:, k * own_half : (k + 1) * own_half] for w in wide], axis=1)
        nat = lax.dot_general(own.astype(BF16), select, NT, preferred_element_type=F32)
        for g in range(groups):
            nat_ref[g, k * block : (k + 1) * block, :] = nat[:, g * LANES : (g + 1) * LANES]
    row = lax.broadcasted_iota(jnp.int32, (16, LANES), 0)
    odd = (row & 1) == 1
    south = (row & 4) == 4
    lane = lax.broadcasted_iota(jnp.int32, (16, LANES), 1)

    for slot in range(slots):
        left = jnp.concatenate(
            [nat_ref[g, pl.ds(slot, 16, stride=slots), :] for g in range(groups)], axis=1
        )
        wait_group(copies, slot)
        sums = lax.dot_general(
            left.astype(BF16), table_ref[slot, :FULL, :], NT, preferred_element_type=F32
        )
        last = jnp.sum(left * table_ref[slot, FULL:PACK, :].astype(F32), axis=1, keepdims=True)
        pair = pairs_ref[first + slot]
        for j in range(TILES):
            mask, sign = slot_masks(pair, lane + j * LANES, odd)
            if j < TILES - 1:
                part = sums[:, j * LANES : (j + 1) * LANES]
            else:
                part = jnp.where(lane == 0, last, 0.0)
            part = part * mask * jnp.where(south, sign, 1.0)
            for g in range(2):
                both = part[g * 8 : g * 8 + 4] + part[g * 8 + 4 : g * 8 + 8]
                tile = jnp.concatenate([both[0:1] + both[1:2], both[2:3] + both[3:4]], axis=0)
                width = min(LANES, PACK - j * LANES)
                out_ref[g * slots + slot, :, j * LANES : j * LANES + width] = tile[:, :width]


def call(kernel, name, out_shape, operands, scratch=(), scalars=0):
    operands = [
        x if i < scalars else pltpu.with_memory_space_constraint(x, pltpu.VMEM)
        for i, x in enumerate(operands)
    ]
    return pl.pallas_call(
        kernel,
        out_shape=tuple(pltpu.VMEM(shape, dtype) for shape, dtype in out_shape),
        in_specs=[
            pl.BlockSpec(memory_space=pltpu.SMEM if i < scalars else pltpu.VMEM)
            for i in range(len(operands))
        ],
        out_specs=(pl.BlockSpec(memory_space=pltpu.VMEM),) * len(out_shape),
        scratch_shapes=scratch,
        compiler_params=pltpu.CompilerParams(vmem_limit_bytes=SCOPED),
        name=name,
    )(*operands)


def two_parts(matrix):
    upper = jnp.asarray(matrix).astype(BF16)
    return upper, (matrix - upper.astype(F32)).astype(BF16)


def trig_table(pair_slots, owners, slot_dev, matrices):
    pairs = pair_slots.reshape(owners, 1, slot_dev)
    orders = jnp.concatenate([pairs, LMAX - pairs], axis=1).reshape(-1, 1)
    span = lax.broadcasted_iota(jnp.int32, (1, LANES), 1)
    coarse = (orders * (span * LANES)) % NPHI
    fine = (orders * span) % NPHI
    scale = 2.0 * math.pi / NPHI
    coarse = coarse.astype(F32) * scale
    fine = fine.astype(F32) * scale
    shape = (2 * orders.shape[0], NPHI)
    trig = (jnp.cos(coarse), jnp.sin(coarse), jnp.cos(fine), jnp.sin(fine))
    made = [(shape, BF16)] + [(m.shape, BF16) for m in matrices]
    return call(table_kernel, "table", made, trig + matrices)


def local(spectra, legendre, pair_slots, theta_owner):
    slot_dev, _, half = legendre.shape
    owners = lax.axis_size("ma")
    levels = lax.axis_size("row") * spectra.shape[0]
    theta_dev = 2 * half // owners
    groups = half // LANES
    synth_upper, synth_lower = two_parts(chebyshev_pair(levels)[0])
    upper, lower = two_parts(chebyshev_pair(levels)[1])
    matrices = (
        jnp.concatenate([synth_upper, synth_lower], axis=1),
        jnp.concatenate([upper, upper, lower], axis=1),
    )
    made = trig_table(pair_slots, owners, slot_dev, matrices)
    orders = made[0].shape[0]
    theta_row = theta_owner.reshape(1, half)

    vmem = pl.BlockSpec(memory_space=pltpu.VMEM)
    smem = pl.BlockSpec(memory_space=pltpu.SMEM)
    far = pl.BlockSpec(memory_space=pltpu.HBM)
    held = [pltpu.VMEM(legendre.shape, BF16), pltpu.SemaphoreType.DMA((slot_dev,))]
    params = pltpu.CompilerParams(vmem_limit_bytes=LEGENDRE_SCOPED)
    near = lambda x: pltpu.with_memory_space_constraint(x, pltpu.VMEM)

    flat = jnp.transpose(spectra, (0, 1, 2, 4, 3)).reshape(3 * slot_dev, 2, PACK)
    (outgoing,) = pl.pallas_call(
        synthesis_kernel,
        out_shape=(pltpu.VMEM((owners, 6 * slot_dev, LANES), BF16),),
        in_specs=[smem, far, vmem, vmem],
        out_specs=(vmem,),
        scratch_shapes=[pltpu.VMEM((groups, 24 * slot_dev, LANES), F32)] + held,
        compiler_params=params,
        name="synthesis",
    )(pair_slots, legendre, near(flat), near(theta_row))
    rows = lax.all_to_all(outgoing, "ma", split_axis=0, concat_axis=0, tiled=True)
    rows, made = lax.optimization_barrier((rows, made))

    full, rest = divmod(orders, LANES)
    sent = -(-(3 * full + 1) // 2)
    assert 3 * rest <= LANES and 2 * rest <= LANES and theta_dev == levels
    (tiles,) = call(
        turn_kernel,
        "turn",
        [((theta_dev * sent, 2, LANES), BF16)],
        (rows,),
        [pltpu.VMEM((theta_dev * sent * 2, LANES), F32)],
    )
    tiles = lax.all_to_all(tiles, "row", split_axis=0, concat_axis=0, tiled=True)
    taken = -(-(2 * full + 1) // 2)
    back = taken + NPHI // LANES
    (tiles,) = call(
        grid_kernel,
        "grid",
        [((levels * back, 2, LANES), BF16)],
        (tiles,) + tuple(made),
        [
            pltpu.VMEM((levels * sent * 2, LANES), F32),
            pltpu.VMEM((3 * levels, orders), BF16),
            pltpu.VMEM((2 * levels, NPHI), BF16),
            pltpu.VMEM((levels * back * 2, LANES), F32),
        ],
    )
    tiles = lax.all_to_all(tiles, "row", split_axis=0, concat_axis=0, tiled=True)
    (fourier,) = call(
        return_kernel,
        "return",
        [((owners, 4 * slot_dev, 2 * theta_dev), BF16)],
        (tiles,),
        [
            pltpu.VMEM((theta_dev * taken * 2, LANES), F32),
            pltpu.VMEM((orders, 2 * theta_dev), F32),
        ],
    )
    flux = pl.pallas_call(
        flux_kernel,
        out_shape=jax.ShapeDtypeStruct((theta_dev, 2, NPHI), BF16),
        in_specs=[vmem],
        compiler_params=pltpu.CompilerParams(vmem_limit_bytes=SCOPED),
        name="flux",
    )(near(tiles))
    returned = lax.all_to_all(fourier, "ma", split_axis=0, concat_axis=0, tiled=True)
    returned, flux = lax.optimization_barrier((returned, flux))
    result = pl.pallas_call(
        analysis_kernel,
        out_shape=jax.ShapeDtypeStruct((2 * slot_dev, 2, PACK), F32),
        in_specs=[smem, far, vmem, vmem],
        scratch_shapes=[pltpu.VMEM((groups, 16 * slot_dev, LANES), F32)] + held,
        compiler_params=params,
        name="analysis",
    )(pair_slots, legendre, near(returned), near(theta_row))
    result = jnp.transpose(result.reshape(1, 2, slot_dev, 2, PACK), (0, 1, 2, 4, 3))
    return flux[None], result


def solution(mesh):
    in_specs = (P("row", None, "ma", None, None), P("ma", None, None), P(), P())
    out_specs = (P("row", "ma", None, None), P("row", None, "ma", None, None))
    return jax.shard_map(local, mesh=mesh, in_specs=in_specs, out_specs=out_specs, check_vma=False)
```

```python
import math

import jax
import jax.numpy as jnp
import numpy as np
from jax import lax
from jax.experimental import pallas as pl
from jax.experimental.pallas import tpu as pltpu
from jax.sharding import PartitionSpec as P

LMAX = 511
NPHI = 1536
NPAIRS = 256
PACK = 513
LANES = 128
TILES = -(-PACK // LANES)
FULL = PACK // LANES * LANES
WIDTH = 256
SCOPED = 16 << 20
LEGENDRE_SCOPED = 56 << 20
SYNTHESIS_SCOPED = 65300 << 10
GROUP = 4
AHEAD = 8
BF16 = jnp.bfloat16
F32 = jnp.float32
NT = (((1,), (1,)), ((), ()))


def chebyshev_pair(levels):
    index = np.arange(levels)
    cosines = np.cos(np.pi * (np.outer(index, index) % (2 * (levels - 1))) / (levels - 1))
    ends = np.where((index == 0) | (index == levels - 1), 0.5, 1.0)
    analysis = (2.0 / (levels - 1)) ** 0.5 * np.outer(ends, ends) * cosines
    return cosines.astype(np.float32), analysis.astype(np.float32)


def one_hot(theta):
    half = theta.shape[0]
    natural = lax.broadcasted_iota(jnp.int32, (half, half), 0)
    return jnp.where(natural == theta.reshape(1, half), 1.0, 0.0).astype(BF16)


def slot_masks(pair, column, order_odd):
    used = pair < NPAIRS
    low = jnp.where(used & (column <= LMAX - pair), 1.0, 0.0)
    high = jnp.where(used & (column > LMAX - pair), 1.0, 0.0)
    low_sign = (1 - 2 * (column & 1)).astype(F32)
    high_sign = (1 - 2 * ((column + pair) & 1)).astype(F32)
    return jnp.where(order_odd, high, low), jnp.where(order_odd, high_sign, low_sign)


def slot_copies(source_ref, table_ref, arrived):
    copies = [
        pltpu.make_async_copy(source_ref.at[slot], table_ref.at[slot], arrived.at[slot])
        for slot in range(table_ref.shape[0])
    ]
    for copy in copies[:AHEAD]:
        copy.start()
    return copies


def wait_group(copies, slot):
    if slot == 0 or (slot - 2) % GROUP == 0:
        end = slot + GROUP if slot else 2
        for copy in copies[slot:end]:
            copy.wait()
        for copy in copies[slot + AHEAD : end + AHEAD]:
            copy.start()


def synthesis_kernel(
    pairs_ref, source_ref, given_ref, owner_ref, out_ref,
    rows_ref, spectra_ref, theta_ref, here, table_ref, arrived,
):
    slots = table_ref.shape[0]
    given = pltpu.make_async_copy(given_ref, spectra_ref, here.at[0])
    owner = pltpu.make_async_copy(owner_ref, theta_ref, here.at[1])
    given.start()
    owner.start()
    copies = slot_copies(source_ref, table_ref, arrived)
    first = lax.axis_index("ma") * slots
    owners = out_ref.shape[0]
    own_half = theta_ref.shape[0] // owners
    groups = rows_ref.shape[0]
    block = 6 * slots
    row = lax.broadcasted_iota(jnp.int32, (8, LANES), 0)
    odd = (row & 1) == 1
    field = row >> 1
    lane = lax.broadcasted_iota(jnp.int32, (8, LANES), 1)

    for slot in range(slots):
        if slot == 0:
            given.wait()
            owner.wait()
        wait_group(copies, slot)
        pair = pairs_ref[first + slot]
        weight = jnp.where((pair == 0) & (row & 1 == 0), 1.0, 2.0)
        blocks = [[], [], [], []]
        for j in range(TILES):
            picked = [f * slots + slot for f in range(3)]
            if j < TILES - 1:
                tiles = [spectra_ref[i, :, j * LANES : (j + 1) * LANES] for i in picked]
            else:
                tiles = [
                    jnp.broadcast_to(spectra_ref[i, :, FULL:PACK], (2, LANES)) for i in picked
                ]
            mask, sign = slot_masks(pair, lane + j * LANES, odd)
            mask = mask * weight
            for c in range(2):
                parts = [jnp.broadcast_to(t[c : c + 1], (8, LANES)) for t in tiles]
                base = jnp.where(field == 0, parts[0], jnp.where(field == 1, parts[1], parts[2]))
                base = base * mask
                blocks[2 * c].append(base)
                blocks[2 * c + 1].append(base * sign)
        left = jnp.concatenate([jnp.concatenate(b, axis=1) for b in blocks], axis=0)
        sums = jnp.dot(
            left[:, :FULL].astype(BF16), table_ref[slot, :FULL, :], preferred_element_type=F32
        )
        sums = sums + left[:, FULL : FULL + 1] * table_ref[slot, FULL:PACK, :].astype(F32)
        for k in range(4):
            for g in range(groups):
                rows_ref[g, pl.ds(k * block + slot, 6, stride=slots), :] = sums[
                    k * 8 : k * 8 + 6, g * LANES : (g + 1) * LANES
                ]
    select = one_hot(theta_ref[...])
    moved = []
    for k in range(4):
        rows = jnp.concatenate(
            [rows_ref[g, k * block : (k + 1) * block, :] for g in range(groups)], axis=1
        ).astype(BF16)
        moved.append(jnp.dot(rows, select, preferred_element_type=F32))
    for d in range(owners):
        out_ref[d] = jnp.concatenate(
            [m[:, d * own_half : (d + 1) * own_half] for m in moved], axis=1
        ).astype(BF16)


def table_kernel(
    coarse_cos_ref, coarse_sin_ref, fine_cos_ref, fine_sin_ref, synth_ref, analysis_ref,
    out_ref, kept_synth_ref, kept_analysis_ref,
):
    kept_synth_ref[...] = synth_ref[...]
    kept_analysis_ref[...] = analysis_ref[...]
    rows = fine_cos_ref.shape[0]
    fine_cos = fine_cos_ref[...]
    fine_sin = fine_sin_ref[...]
    for a in range(NPHI // LANES):
        cos_a = coarse_cos_ref[:, a : a + 1]
        sin_a = coarse_sin_ref[:, a : a + 1]
        span = slice(a * LANES, (a + 1) * LANES)
        out_ref[:rows, span] = (cos_a * fine_cos - sin_a * fine_sin).astype(BF16)
        out_ref[rows:, span] = (-(sin_a * fine_cos + cos_a * fine_sin)).astype(BF16)


def scatter_row(wide_ref, row, rows, value):
    wide_ref[pl.ds(row, value.shape[0], stride=rows), :] = value


def scatter_rows(wide_ref, row, rows, values):
    full = values[0].shape[1] // LANES
    for value in values:
        for j in range(full):
            scatter_row(wide_ref, row, rows, value[:, j * LANES : (j + 1) * LANES])
            row += 1
    rest = [value[:, full * LANES :] for value in values]
    filled = sum(r.shape[1] for r in rest)
    rest.append(jnp.zeros((rest[0].shape[0], LANES - filled), F32))
    scatter_row(wide_ref, row, rows, jnp.concatenate(rest, axis=1))
    scatter_row(wide_ref, row + 1, rows, jnp.zeros_like(values[0][:, :LANES]))


def gather_rows(wide_ref, count, rows, arrays, width):
    full = width // LANES
    line = lambda row: wide_ref[pl.ds(row, count, stride=rows), :]
    rest = line(arrays * full)
    part = width - full * LANES
    return [
        jnp.concatenate(
            [line(a * full + j) for j in range(full)] + [rest[:, a * part : (a + 1) * part]],
            axis=1,
        )
        for a in range(arrays)
    ]


def widen(tiles_ref, wide_ref, count, stride, taken):
    for i in range(count):
        for t in range(taken):
            line = 2 * (i * taken + t)
            wide_ref[line : line + 2, :] = tiles_ref[i * stride + t].astype(F32)


def narrow(wide_ref, tiles_ref):
    for t in range(tiles_ref.shape[0]):
        tiles_ref[t] = wide_ref[2 * t : 2 * t + 2, :].astype(BF16)


def turn_kernel(rows_ref, out_ref, wide_ref):
    owners = rows_ref.shape[0]
    part = rows_ref.shape[1] // 3
    theta = rows_ref.shape[2] // 2
    wide = [rows_ref[d].astype(F32) for d in range(owners)]
    lines = []
    for f in range(3):
        turned = jnp.concatenate([w[f * part : (f + 1) * part] for w in wide], axis=0).T
        lines.append(jnp.concatenate([turned[:theta], turned[theta:]], axis=1))
    scatter_rows(wide_ref, 0, wide_ref.shape[0] // theta, lines)
    narrow(wide_ref, out_ref)


def grid_kernel(
    tiles_ref, table_ref, synth_ref, analysis_ref, out_ref, wide_ref, left_ref, both_ref, out_wide_ref
):
    levels = synth_ref.shape[0]
    orders = table_ref.shape[0]
    per_level = tiles_ref.shape[0] // levels
    widen(tiles_ref, wide_ref, levels, per_level, per_level)
    for f, line in enumerate(gather_rows(wide_ref, levels, 2 * per_level, 3, orders)):
        line = line.astype(BF16)
        left_ref[f * levels : (f + 1) * levels, :] = jnp.dot(
            synth_ref[...], jnp.concatenate([line, line], axis=0), preferred_element_type=F32
        ).astype(BF16)
    rows = out_wide_ref.shape[0] // levels
    flux_row = rows - 2 * NPHI // LANES
    for q in range(NPHI // WIDTH):
        span = slice(q * WIDTH, (q + 1) * WIDTH)
        grid = jnp.dot(left_ref[...], table_ref[:, span], preferred_element_type=F32)
        for g in range(2):
            flux = (grid[:levels] * grid[(1 + g) * levels : (2 + g) * levels]).astype(BF16)
            both_ref[g * levels : (g + 1) * levels, span] = flux
            flux = flux.astype(F32)
            for j in range(WIDTH // LANES):
                row = flux_row + 2 * (q * (WIDTH // LANES) + j) + g
                scatter_row(out_wide_ref, row, rows, flux[:, j * LANES : (j + 1) * LANES])
    fourier = lax.dot_general(
        both_ref[...], table_ref[...], NT, preferred_element_type=F32
    ) * NPHI ** (-0.5)
    mixed = []
    for g in range(2):
        value = fourier[g * levels : (g + 1) * levels]
        upper = value.astype(BF16)
        lower = (value - upper.astype(F32)).astype(BF16)
        right = jnp.concatenate([upper, lower, upper], axis=0)
        mixed.append(jnp.dot(analysis_ref[...], right, preferred_element_type=F32))
    scatter_rows(out_wide_ref, 0, rows, mixed)
    narrow(out_wide_ref, out_ref)


def return_kernel(tiles_ref, out_ref, wide_ref, sum_ref):
    owners = out_ref.shape[0]
    part = out_ref.shape[1] // 2
    orders = 2 * owners * part
    theta = out_ref.shape[2] // 2
    taken = wide_ref.shape[0] // (2 * theta)
    widen(tiles_ref, wide_ref, theta, tiles_ref.shape[0] // theta, taken)
    lines = gather_rows(wide_ref, theta, 2 * taken, 2, orders)
    sum_ref[...] = jnp.concatenate(lines, axis=0).T
    for d in range(owners):
        out_ref[d] = jnp.concatenate(
            [
                sum_ref[c * owners * part + d * part : c * owners * part + (d + 1) * part, :]
                for c in range(2)
            ],
            axis=0,
        ).astype(BF16)


def flux_kernel(tiles_ref, out_ref):
    theta = out_ref.shape[0]
    stride = tiles_ref.shape[0] // theta
    count = NPHI // LANES
    for t in range(theta):
        for q in range(count):
            out_ref[t, :, q * LANES : (q + 1) * LANES] = tiles_ref[t * stride + stride - count + q]


def analysis_kernel(
    pairs_ref, source_ref, rows_ref, theta_ref, out_ref, nat_ref, table_ref, arrived
):
    slots = table_ref.shape[0]
    copies = slot_copies(source_ref, table_ref, arrived)
    first = lax.axis_index("ma") * slots
    owners = rows_ref.shape[0]
    own_half = theta_ref.shape[0] // owners
    block = rows_ref.shape[1]
    groups = nat_ref.shape[0]
    select = one_hot(theta_ref[...])
    wide = [rows_ref[d].astype(F32) for d in range(owners)]
    for k in range(4):
        own = jnp.concatenate([w[:, k * own_half : (k + 1) * own_half] for w in wide], axis=1)
        nat = lax.dot_general(own.astype(BF16), select, NT, preferred_element_type=F32)
        for g in range(groups):
            nat_ref[g, k * block : (k + 1) * block, :] = nat[:, g * LANES : (g + 1) * LANES]
    row = lax.broadcasted_iota(jnp.int32, (16, LANES), 0)
    odd = (row & 1) == 1
    south = (row & 4) == 4
    lane = lax.broadcasted_iota(jnp.int32, (16, LANES), 1)

    for slot in range(slots):
        left = jnp.concatenate(
            [nat_ref[g, pl.ds(slot, 16, stride=slots), :] for g in range(groups)], axis=1
        )
        wait_group(copies, slot)
        sums = lax.dot_general(
            left.astype(BF16), table_ref[slot, :FULL, :], NT, preferred_element_type=F32
        )
        last = jnp.sum(left * table_ref[slot, FULL:PACK, :].astype(F32), axis=1, keepdims=True)
        pair = pairs_ref[first + slot]
        for j in range(TILES):
            mask, sign = slot_masks(pair, lane + j * LANES, odd)
            if j < TILES - 1:
                part = sums[:, j * LANES : (j + 1) * LANES]
            else:
                part = jnp.where(lane == 0, last, 0.0)
            part = part * mask * jnp.where(south, sign, 1.0)
            for g in range(2):
                both = part[g * 8 : g * 8 + 4] + part[g * 8 + 4 : g * 8 + 8]
                tile = jnp.concatenate([both[0:1] + both[1:2], both[2:3] + both[3:4]], axis=0)
                width = min(LANES, PACK - j * LANES)
                out_ref[g * slots + slot, :, j * LANES : j * LANES + width] = tile[:, :width]


def call(kernel, name, out_shape, operands, scratch=(), scalars=0):
    operands = [
        x if i < scalars else pltpu.with_memory_space_constraint(x, pltpu.VMEM)
        for i, x in enumerate(operands)
    ]
    return pl.pallas_call(
        kernel,
        out_shape=tuple(pltpu.VMEM(shape, dtype) for shape, dtype in out_shape),
        in_specs=[
            pl.BlockSpec(memory_space=pltpu.SMEM if i < scalars else pltpu.VMEM)
            for i in range(len(operands))
        ],
        out_specs=(pl.BlockSpec(memory_space=pltpu.VMEM),) * len(out_shape),
        scratch_shapes=scratch,
        compiler_params=pltpu.CompilerParams(vmem_limit_bytes=SCOPED),
        name=name,
    )(*operands)


def two_parts(matrix):
    upper = jnp.asarray(matrix).astype(BF16)
    return upper, (matrix - upper.astype(F32)).astype(BF16)


def trig_table(pair_slots, owners, slot_dev, matrices):
    pairs = pair_slots.reshape(owners, 1, slot_dev)
    orders = jnp.concatenate([pairs, LMAX - pairs], axis=1).reshape(-1, 1)
    span = lax.broadcasted_iota(jnp.int32, (1, LANES), 1)
    coarse = (orders * (span * LANES)) % NPHI
    fine = (orders * span) % NPHI
    scale = 2.0 * math.pi / NPHI
    coarse = coarse.astype(F32) * scale
    fine = fine.astype(F32) * scale
    shape = (2 * orders.shape[0], NPHI)
    trig = (jnp.cos(coarse), jnp.sin(coarse), jnp.cos(fine), jnp.sin(fine))
    made = [(shape, BF16)] + [(m.shape, BF16) for m in matrices]
    return call(table_kernel, "table", made, trig + matrices)


def local(spectra, legendre, pair_slots, theta_owner):
    slot_dev, _, half = legendre.shape
    owners = lax.axis_size("ma")
    levels = lax.axis_size("row") * spectra.shape[0]
    theta_dev = 2 * half // owners
    groups = half // LANES
    synth_upper, synth_lower = two_parts(chebyshev_pair(levels)[0])
    upper, lower = two_parts(chebyshev_pair(levels)[1])
    matrices = (
        jnp.concatenate([synth_upper, synth_lower], axis=1),
        jnp.concatenate([upper, upper, lower], axis=1),
    )
    made = trig_table(pair_slots, owners, slot_dev, matrices)
    orders = made[0].shape[0]

    vmem = pl.BlockSpec(memory_space=pltpu.VMEM)
    smem = pl.BlockSpec(memory_space=pltpu.SMEM)
    far = pl.BlockSpec(memory_space=pltpu.HBM)
    held = [pltpu.VMEM(legendre.shape, BF16), pltpu.SemaphoreType.DMA((slot_dev,))]
    params = pltpu.CompilerParams(vmem_limit_bytes=LEGENDRE_SCOPED)
    near = lambda x: pltpu.with_memory_space_constraint(x, pltpu.VMEM)

    flat = jnp.transpose(spectra, (0, 1, 2, 4, 3)).reshape(3 * slot_dev, 2, PACK)
    outgoing = pl.pallas_call(
        synthesis_kernel,
        out_shape=jax.ShapeDtypeStruct((owners, 6 * slot_dev, LANES), BF16),
        in_specs=[smem, far, far, far],
        scratch_shapes=[
            pltpu.VMEM((groups, 24 * slot_dev, LANES), F32),
            pltpu.VMEM(flat.shape, F32),
            pltpu.VMEM(theta_owner.shape, jnp.int32),
            pltpu.SemaphoreType.DMA((2,)),
        ]
        + held,
        compiler_params=pltpu.CompilerParams(vmem_limit_bytes=SYNTHESIS_SCOPED),
        name="synthesis",
    )(pair_slots, legendre, flat, theta_owner)
    rows = lax.all_to_all(outgoing, "ma", split_axis=0, concat_axis=0, tiled=True)
    rows, made = lax.optimization_barrier((rows, made))

    full, rest = divmod(orders, LANES)
    sent = -(-(3 * full + 1) // 2)
    assert 3 * rest <= LANES and 2 * rest <= LANES and theta_dev == levels
    (tiles,) = call(
        turn_kernel,
        "turn",
        [((theta_dev * sent, 2, LANES), BF16)],
        (rows,),
        [pltpu.VMEM((theta_dev * sent * 2, LANES), F32)],
    )
    tiles = lax.all_to_all(tiles, "row", split_axis=0, concat_axis=0, tiled=True)
    taken = -(-(2 * full + 1) // 2)
    back = taken + NPHI // LANES
    (tiles,) = call(
        grid_kernel,
        "grid",
        [((levels * back, 2, LANES), BF16)],
        (tiles,) + tuple(made),
        [
            pltpu.VMEM((levels * sent * 2, LANES), F32),
            pltpu.VMEM((3 * levels, orders), BF16),
            pltpu.VMEM((2 * levels, NPHI), BF16),
            pltpu.VMEM((levels * back * 2, LANES), F32),
        ],
    )
    tiles = lax.all_to_all(tiles, "row", split_axis=0, concat_axis=0, tiled=True)
    (fourier,) = call(
        return_kernel,
        "return",
        [((owners, 4 * slot_dev, 2 * theta_dev), BF16)],
        (tiles,),
        [
            pltpu.VMEM((theta_dev * taken * 2, LANES), F32),
            pltpu.VMEM((orders, 2 * theta_dev), F32),
        ],
    )
    flux = pl.pallas_call(
        flux_kernel,
        out_shape=jax.ShapeDtypeStruct((theta_dev, 2, NPHI), BF16),
        in_specs=[vmem],
        compiler_params=pltpu.CompilerParams(vmem_limit_bytes=SCOPED),
        name="flux",
    )(near(tiles))
    returned = lax.all_to_all(fourier, "ma", split_axis=0, concat_axis=0, tiled=True)
    returned, flux = lax.optimization_barrier((returned, flux))
    result = pl.pallas_call(
        analysis_kernel,
        out_shape=jax.ShapeDtypeStruct((2 * slot_dev, 2, PACK), F32),
        in_specs=[smem, far, vmem, vmem],
        scratch_shapes=[pltpu.VMEM((groups, 16 * slot_dev, LANES), F32)] + held,
        compiler_params=params,
        name="analysis",
    )(pair_slots, legendre, near(returned), near(theta_owner))
    result = jnp.transpose(result.reshape(1, 2, slot_dev, 2, PACK), (0, 1, 2, 4, 3))
    return flux[None], result


def solution(mesh):
    in_specs = (P("row", None, "ma", None, None), P("ma", None, None), P(), P())
    out_specs = (P("row", "ma", None, None), P("row", None, "ma", None, None))
    return jax.shard_map(local, mesh=mesh, in_specs=in_specs, out_specs=out_specs, check_vma=False)
```

```python
import math

import jax
import jax.numpy as jnp
import numpy as np
from jax import lax
from jax.experimental import pallas as pl
from jax.experimental.pallas import tpu as pltpu
from jax.sharding import PartitionSpec as P

LMAX = 511
NPHI = 1536
NPAIRS = 256
PACK = 513
LANES = 128
TILES = -(-PACK // LANES)
FULL = PACK // LANES * LANES
WIDTH = 256
SCOPED = 16 << 20
LEGENDRE_SCOPED = 56 << 20
SYNTHESIS_SCOPED = 65300 << 10
GROUP = 4
FIRST = 6
BF16 = jnp.bfloat16
F32 = jnp.float32
NT = (((1,), (1,)), ((), ()))


def chebyshev_pair(levels):
    index = np.arange(levels)
    cosines = np.cos(np.pi * (np.outer(index, index) % (2 * (levels - 1))) / (levels - 1))
    ends = np.where((index == 0) | (index == levels - 1), 0.5, 1.0)
    analysis = (2.0 / (levels - 1)) ** 0.5 * np.outer(ends, ends) * cosines
    return cosines.astype(np.float32), analysis.astype(np.float32)


def one_hot(theta):
    half = theta.shape[0]
    natural = lax.broadcasted_iota(jnp.int32, (half, half), 0)
    return jnp.where(natural == theta.reshape(1, half), 1.0, 0.0).astype(BF16)


def slot_masks(pair, column, order_odd):
    used = pair < NPAIRS
    low = jnp.where(used & (column <= LMAX - pair), 1.0, 0.0)
    high = jnp.where(used & (column > LMAX - pair), 1.0, 0.0)
    low_sign = (1 - 2 * (column & 1)).astype(F32)
    high_sign = (1 - 2 * ((column + pair) & 1)).astype(F32)
    return jnp.where(order_odd, high, low), jnp.where(order_odd, high_sign, low_sign)


def slot_copies(source_ref, table_ref, arrived):
    copies = [
        pltpu.make_async_copy(source_ref.at[slot], table_ref.at[slot], arrived.at[slot])
        for slot in range(table_ref.shape[0])
    ]
    for copy in copies[:FIRST]:
        copy.start()
    return copies


def slot_groups(slots):
    return [(0, 2)] + [(s, min(s + GROUP, slots)) for s in range(2, slots, GROUP)]


def synthesis_kernel(
    pairs_ref, source_ref, given_ref, owner_ref, result_ref,
    rows_ref, spectra_ref, theta_ref, here, out_ref, gone, table_ref, arrived,
):
    slots = table_ref.shape[0]
    given = pltpu.make_async_copy(given_ref, spectra_ref, here.at[0])
    owner = pltpu.make_async_copy(owner_ref, theta_ref, here.at[1])
    given.start()
    owner.start()
    copies = slot_copies(source_ref, table_ref, arrived)
    first = lax.axis_index("ma") * slots
    owners = out_ref.shape[0]
    own_half = theta_ref.shape[0] // owners
    groups = rows_ref.shape[0]
    block = 6 * slots
    row = lax.broadcasted_iota(jnp.int32, (8, LANES), 0)
    odd = (row & 1) == 1
    field = row >> 1
    lane = lax.broadcasted_iota(jnp.int32, (8, LANES), 1)

    def left_of(slot):
        pair = pairs_ref[first + slot]
        weight = jnp.where((pair == 0) & (row & 1 == 0), 1.0, 2.0)
        blocks = [[], [], [], []]
        picked = [f * slots + slot for f in range(3)]
        for j in range(TILES):
            if j < TILES - 1:
                tiles = [spectra_ref[i, :, j * LANES : (j + 1) * LANES] for i in picked]
            else:
                tiles = [
                    jnp.broadcast_to(spectra_ref[i, :, FULL:PACK], (2, LANES)) for i in picked
                ]
            mask, sign = slot_masks(pair, lane + j * LANES, odd)
            mask = mask * weight
            for c in range(2):
                parts = [jnp.broadcast_to(t[c : c + 1], (8, LANES)) for t in tiles]
                base = jnp.where(field == 0, parts[0], jnp.where(field == 1, parts[1], parts[2]))
                base = base * mask
                blocks[2 * c].append(base)
                blocks[2 * c + 1].append(base * sign)
        left = jnp.concatenate([jnp.concatenate(b, axis=1) for b in blocks], axis=0)
        return left[:, :FULL].astype(BF16), left[:, FULL : FULL + 1]

    def sums_of(slot, left):
        sums = jnp.dot(left[0], table_ref[slot, :FULL, :], preferred_element_type=F32)
        return sums + left[1] * table_ref[slot, FULL:PACK, :].astype(F32)

    def keep(slot, sums):
        for k in range(4):
            for g in range(groups):
                rows_ref[g, pl.ds(k * block + slot, 6, stride=slots), :] = sums[
                    k * 8 : k * 8 + 6, g * LANES : (g + 1) * LANES
                ]

    given.wait()
    owner.wait()
    for copy in copies[FIRST:]:
        copy.start()
    batches = slot_groups(slots)
    lefts = [left_of(slot) for slot in range(*batches[0])]
    select = one_hot(theta_ref[...])
    done = []
    for number, (start, end) in enumerate(batches):
        for copy in copies[start:end]:
            copy.wait()
        made = [(slot, sums_of(slot, lefts[slot - start])) for slot in range(start, end)]
        if number + 1 < len(batches):
            lefts = [left_of(slot) for slot in range(*batches[number + 1])]
        for slot, sums in done:
            keep(slot, sums)
        done = made
    for slot, sums in done:
        keep(slot, sums)
    moved = []
    for k in range(4):
        rows = jnp.concatenate(
            [rows_ref[g, k * block : (k + 1) * block, :] for g in range(groups)], axis=1
        ).astype(BF16)
        moved.append(jnp.dot(rows, select, preferred_element_type=F32))
    sent = []
    for d in range(owners):
        out_ref[d] = jnp.concatenate(
            [m[:, d * own_half : (d + 1) * own_half] for m in moved], axis=1
        ).astype(BF16)
        sent.append(pltpu.make_async_copy(out_ref.at[d], result_ref.at[d], gone.at[d]))
        sent[-1].start()
    for copy in sent:
        copy.wait()


def table_kernel(
    coarse_cos_ref, coarse_sin_ref, fine_cos_ref, fine_sin_ref, synth_ref, analysis_ref,
    out_ref, kept_synth_ref, kept_analysis_ref,
):
    kept_synth_ref[...] = synth_ref[...]
    kept_analysis_ref[...] = analysis_ref[...]
    rows = fine_cos_ref.shape[0]
    fine_cos = fine_cos_ref[...]
    fine_sin = fine_sin_ref[...]
    for a in range(NPHI // LANES):
        cos_a = coarse_cos_ref[:, a : a + 1]
        sin_a = coarse_sin_ref[:, a : a + 1]
        span = slice(a * LANES, (a + 1) * LANES)
        out_ref[:rows, span] = (cos_a * fine_cos - sin_a * fine_sin).astype(BF16)
        out_ref[rows:, span] = (-(sin_a * fine_cos + cos_a * fine_sin)).astype(BF16)


def scatter_row(wide_ref, row, rows, value):
    wide_ref[pl.ds(row, value.shape[0], stride=rows), :] = value


def scatter_rows(wide_ref, row, rows, values):
    full = values[0].shape[1] // LANES
    for value in values:
        for j in range(full):
            scatter_row(wide_ref, row, rows, value[:, j * LANES : (j + 1) * LANES])
            row += 1
    rest = [value[:, full * LANES :] for value in values]
    filled = sum(r.shape[1] for r in rest)
    rest.append(jnp.zeros((rest[0].shape[0], LANES - filled), F32))
    scatter_row(wide_ref, row, rows, jnp.concatenate(rest, axis=1))
    scatter_row(wide_ref, row + 1, rows, jnp.zeros_like(values[0][:, :LANES]))


def gather_rows(wide_ref, count, rows, arrays, width):
    full = width // LANES
    line = lambda row: wide_ref[pl.ds(row, count, stride=rows), :]
    rest = line(arrays * full)
    part = width - full * LANES
    return [
        jnp.concatenate(
            [line(a * full + j) for j in range(full)] + [rest[:, a * part : (a + 1) * part]],
            axis=1,
        )
        for a in range(arrays)
    ]


def widen(tiles_ref, wide_ref, count, stride, taken):
    for i in range(count):
        for t in range(taken):
            line = 2 * (i * taken + t)
            wide_ref[line : line + 2, :] = tiles_ref[i * stride + t].astype(F32)


def narrow(wide_ref, tiles_ref):
    for t in range(tiles_ref.shape[0]):
        tiles_ref[t] = wide_ref[2 * t : 2 * t + 2, :].astype(BF16)


def turn_kernel(rows_ref, out_ref, wide_ref):
    owners = rows_ref.shape[0]
    part = rows_ref.shape[1] // 3
    theta = rows_ref.shape[2] // 2
    wide = [rows_ref[d].astype(F32) for d in range(owners)]
    lines = []
    for f in range(3):
        turned = jnp.concatenate([w[f * part : (f + 1) * part] for w in wide], axis=0).T
        lines.append(jnp.concatenate([turned[:theta], turned[theta:]], axis=1))
    scatter_rows(wide_ref, 0, wide_ref.shape[0] // theta, lines)
    narrow(wide_ref, out_ref)


def grid_kernel(
    tiles_ref, table_ref, synth_ref, analysis_ref, out_ref, wide_ref, left_ref, both_ref, out_wide_ref
):
    levels = synth_ref.shape[0]
    orders = table_ref.shape[0]
    per_level = tiles_ref.shape[0] // levels
    widen(tiles_ref, wide_ref, levels, per_level, per_level)
    for f, line in enumerate(gather_rows(wide_ref, levels, 2 * per_level, 3, orders)):
        line = line.astype(BF16)
        left_ref[f * levels : (f + 1) * levels, :] = jnp.dot(
            synth_ref[...], jnp.concatenate([line, line], axis=0), preferred_element_type=F32
        ).astype(BF16)
    rows = out_wide_ref.shape[0] // levels
    flux_row = rows - 2 * NPHI // LANES
    for q in range(NPHI // WIDTH):
        span = slice(q * WIDTH, (q + 1) * WIDTH)
        grid = jnp.dot(left_ref[...], table_ref[:, span], preferred_element_type=F32)
        for g in range(2):
            flux = (grid[:levels] * grid[(1 + g) * levels : (2 + g) * levels]).astype(BF16)
            both_ref[g * levels : (g + 1) * levels, span] = flux
            flux = flux.astype(F32)
            for j in range(WIDTH // LANES):
                row = flux_row + 2 * (q * (WIDTH // LANES) + j) + g
                scatter_row(out_wide_ref, row, rows, flux[:, j * LANES : (j + 1) * LANES])
    fourier = lax.dot_general(
        both_ref[...], table_ref[...], NT, preferred_element_type=F32
    ) * NPHI ** (-0.5)
    mixed = []
    for g in range(2):
        value = fourier[g * levels : (g + 1) * levels]
        upper = value.astype(BF16)
        lower = (value - upper.astype(F32)).astype(BF16)
        right = jnp.concatenate([upper, lower, upper], axis=0)
        mixed.append(jnp.dot(analysis_ref[...], right, preferred_element_type=F32))
    scatter_rows(out_wide_ref, 0, rows, mixed)
    narrow(out_wide_ref, out_ref)


def return_kernel(tiles_ref, out_ref, wide_ref, sum_ref):
    owners = out_ref.shape[0]
    part = out_ref.shape[1] // 2
    orders = 2 * owners * part
    theta = out_ref.shape[2] // 2
    taken = wide_ref.shape[0] // (2 * theta)
    widen(tiles_ref, wide_ref, theta, tiles_ref.shape[0] // theta, taken)
    lines = gather_rows(wide_ref, theta, 2 * taken, 2, orders)
    sum_ref[...] = jnp.concatenate(lines, axis=0).T
    for d in range(owners):
        out_ref[d] = jnp.concatenate(
            [
                sum_ref[c * owners * part + d * part : c * owners * part + (d + 1) * part, :]
                for c in range(2)
            ],
            axis=0,
        ).astype(BF16)


def flux_kernel(tiles_ref, out_ref):
    theta = out_ref.shape[0]
    stride = tiles_ref.shape[0] // theta
    count = NPHI // LANES
    for t in range(theta):
        for q in range(count):
            out_ref[t, :, q * LANES : (q + 1) * LANES] = tiles_ref[t * stride + stride - count + q]


def analysis_kernel(
    pairs_ref, source_ref, rows_ref, theta_ref, result_ref,
    nat_ref, out_ref, gone, table_ref, arrived,
):
    slots = table_ref.shape[0]
    copies = slot_copies(source_ref, table_ref, arrived)
    first = lax.axis_index("ma") * slots
    owners = rows_ref.shape[0]
    own_half = theta_ref.shape[0] // owners
    block = rows_ref.shape[1]
    groups = nat_ref.shape[0]
    select = one_hot(theta_ref[...])
    wide = [rows_ref[d].astype(F32) for d in range(owners)]
    for k in range(4):
        own = jnp.concatenate([w[:, k * own_half : (k + 1) * own_half] for w in wide], axis=1)
        nat = lax.dot_general(own.astype(BF16), select, NT, preferred_element_type=F32)
        for g in range(groups):
            nat_ref[g, k * block : (k + 1) * block, :] = nat[:, g * LANES : (g + 1) * LANES]
    for copy in copies[FIRST:]:
        copy.start()
    sent = []
    row = lax.broadcasted_iota(jnp.int32, (16, LANES), 0)
    odd = (row & 1) == 1
    south = (row & 4) == 4
    lane = lax.broadcasted_iota(jnp.int32, (16, LANES), 1)

    def products(slot):
        left = jnp.concatenate(
            [nat_ref[g, pl.ds(slot, 16, stride=slots), :] for g in range(groups)], axis=1
        )
        sums = lax.dot_general(
            left.astype(BF16), table_ref[slot, :FULL, :], NT, preferred_element_type=F32
        )
        last = jnp.sum(left * table_ref[slot, FULL:PACK, :].astype(F32), axis=1, keepdims=True)
        return sums, last

    def finish(slot, sums, last):
        pair = pairs_ref[first + slot]
        for j in range(TILES):
            mask, sign = slot_masks(pair, lane + j * LANES, odd)
            if j < TILES - 1:
                part = sums[:, j * LANES : (j + 1) * LANES]
            else:
                part = jnp.where(lane == 0, last, 0.0)
            part = part * mask * jnp.where(south, sign, 1.0)
            width = min(LANES, PACK - j * LANES)
            for g in range(2):
                both = part[g * 8 : g * 8 + 4] + part[g * 8 + 4 : g * 8 + 8]
                tile = jnp.concatenate([both[0:1] + both[1:2], both[2:3] + both[3:4]], axis=0)
                out_ref[g * slots + slot, :, j * LANES : j * LANES + width] = tile[:, :width]

    def send(number, start, end):
        for g in range(2):
            part = pl.ds(g * slots + start, end - start)
            copy = pltpu.make_async_copy(
                out_ref.at[part], result_ref.at[part], gone.at[2 * number + g]
            )
            copy.start()
            sent.append(copy)

    batches = slot_groups(slots)
    done = []
    for number, (start, end) in enumerate(batches):
        for copy in copies[start:end]:
            copy.wait()
        made = [(slot, *products(slot)) for slot in range(start, end)]
        for values in done:
            finish(*values)
        if number:
            send(number - 1, *batches[number - 1])
        done = made
    for values in done:
        finish(*values)
    send(len(batches) - 1, *batches[-1])
    for copy in sent:
        copy.wait()


def call(kernel, name, out_shape, operands, scratch=(), scalars=0):
    operands = [
        x if i < scalars else pltpu.with_memory_space_constraint(x, pltpu.VMEM)
        for i, x in enumerate(operands)
    ]
    return pl.pallas_call(
        kernel,
        out_shape=tuple(pltpu.VMEM(shape, dtype) for shape, dtype in out_shape),
        in_specs=[
            pl.BlockSpec(memory_space=pltpu.SMEM if i < scalars else pltpu.VMEM)
            for i in range(len(operands))
        ],
        out_specs=(pl.BlockSpec(memory_space=pltpu.VMEM),) * len(out_shape),
        scratch_shapes=scratch,
        compiler_params=pltpu.CompilerParams(vmem_limit_bytes=SCOPED),
        name=name,
    )(*operands)


def two_parts(matrix):
    upper = jnp.asarray(matrix).astype(BF16)
    return upper, (matrix - upper.astype(F32)).astype(BF16)


def trig_table(pair_slots, owners, slot_dev, matrices):
    pairs = pair_slots.reshape(owners, 1, slot_dev)
    orders = jnp.concatenate([pairs, LMAX - pairs], axis=1).reshape(-1, 1)
    span = lax.broadcasted_iota(jnp.int32, (1, LANES), 1)
    coarse = (orders * (span * LANES)) % NPHI
    fine = (orders * span) % NPHI
    scale = 2.0 * math.pi / NPHI
    coarse = coarse.astype(F32) * scale
    fine = fine.astype(F32) * scale
    shape = (2 * orders.shape[0], NPHI)
    trig = (jnp.cos(coarse), jnp.sin(coarse), jnp.cos(fine), jnp.sin(fine))
    made = [(shape, BF16)] + [(m.shape, BF16) for m in matrices]
    return call(table_kernel, "table", made, trig + matrices)


def local(spectra, legendre, pair_slots, theta_owner):
    slot_dev, _, half = legendre.shape
    owners = lax.axis_size("ma")
    levels = lax.axis_size("row") * spectra.shape[0]
    theta_dev = 2 * half // owners
    groups = half // LANES
    synth_upper, synth_lower = two_parts(chebyshev_pair(levels)[0])
    upper, lower = two_parts(chebyshev_pair(levels)[1])
    matrices = (
        jnp.concatenate([synth_upper, synth_lower], axis=1),
        jnp.concatenate([upper, upper, lower], axis=1),
    )
    made = trig_table(pair_slots, owners, slot_dev, matrices)
    orders = made[0].shape[0]

    vmem = pl.BlockSpec(memory_space=pltpu.VMEM)
    smem = pl.BlockSpec(memory_space=pltpu.SMEM)
    far = pl.BlockSpec(memory_space=pltpu.HBM)
    held = [pltpu.VMEM(legendre.shape, BF16), pltpu.SemaphoreType.DMA((slot_dev,))]
    params = pltpu.CompilerParams(vmem_limit_bytes=LEGENDRE_SCOPED)
    near = lambda x: pltpu.with_memory_space_constraint(x, pltpu.VMEM)

    flat = jnp.transpose(spectra, (0, 1, 2, 4, 3)).reshape(3 * slot_dev, 2, PACK)
    outgoing = pl.pallas_call(
        synthesis_kernel,
        out_shape=jax.ShapeDtypeStruct((owners, 6 * slot_dev, LANES), BF16),
        in_specs=[smem, far, far, far],
        out_specs=far,
        scratch_shapes=[
            pltpu.VMEM((groups, 24 * slot_dev, LANES), F32),
            pltpu.VMEM(flat.shape, F32),
            pltpu.VMEM(theta_owner.shape, jnp.int32),
            pltpu.SemaphoreType.DMA((2,)),
            pltpu.VMEM((owners, 6 * slot_dev, LANES), BF16),
            pltpu.SemaphoreType.DMA((owners,)),
        ]
        + held,
        compiler_params=pltpu.CompilerParams(vmem_limit_bytes=SYNTHESIS_SCOPED),
        name="synthesis",
    )(pair_slots, legendre, flat, theta_owner)
    rows = lax.all_to_all(outgoing, "ma", split_axis=0, concat_axis=0, tiled=True)
    rows, made = lax.optimization_barrier((rows, made))

    full, rest = divmod(orders, LANES)
    sent = -(-(3 * full + 1) // 2)
    assert 3 * rest <= LANES and 2 * rest <= LANES and theta_dev == levels
    (tiles,) = call(
        turn_kernel,
        "turn",
        [((theta_dev * sent, 2, LANES), BF16)],
        (rows,),
        [pltpu.VMEM((theta_dev * sent * 2, LANES), F32)],
    )
    tiles = lax.all_to_all(tiles, "row", split_axis=0, concat_axis=0, tiled=True)
    taken = -(-(2 * full + 1) // 2)
    back = taken + NPHI // LANES
    (tiles,) = call(
        grid_kernel,
        "grid",
        [((levels * back, 2, LANES), BF16)],
        (tiles,) + tuple(made),
        [
            pltpu.VMEM((levels * sent * 2, LANES), F32),
            pltpu.VMEM((3 * levels, orders), BF16),
            pltpu.VMEM((2 * levels, NPHI), BF16),
            pltpu.VMEM((levels * back * 2, LANES), F32),
        ],
    )
    tiles = lax.all_to_all(tiles, "row", split_axis=0, concat_axis=0, tiled=True)
    (fourier,) = call(
        return_kernel,
        "return",
        [((owners, 4 * slot_dev, 2 * theta_dev), BF16)],
        (tiles,),
        [
            pltpu.VMEM((theta_dev * taken * 2, LANES), F32),
            pltpu.VMEM((orders, 2 * theta_dev), F32),
        ],
    )
    flux = pl.pallas_call(
        flux_kernel,
        out_shape=jax.ShapeDtypeStruct((theta_dev, 2, NPHI), BF16),
        in_specs=[vmem],
        compiler_params=pltpu.CompilerParams(vmem_limit_bytes=SCOPED),
        name="flux",
    )(near(tiles))
    returned = lax.all_to_all(fourier, "ma", split_axis=0, concat_axis=0, tiled=True)
    returned, flux = lax.optimization_barrier((returned, flux))
    result = pl.pallas_call(
        analysis_kernel,
        out_shape=jax.ShapeDtypeStruct((2 * slot_dev, 2, PACK), F32),
        in_specs=[smem, far, vmem, vmem],
        out_specs=far,
        scratch_shapes=[
            pltpu.VMEM((groups, 16 * slot_dev, LANES), F32),
            pltpu.VMEM((2 * slot_dev, 2, PACK), F32),
            pltpu.SemaphoreType.DMA((2 * len(slot_groups(slot_dev)),)),
        ]
        + held,
        compiler_params=params,
        name="analysis",
    )(pair_slots, legendre, near(returned), near(theta_owner))
    result = jnp.transpose(result.reshape(1, 2, slot_dev, 2, PACK), (0, 1, 2, 4, 3))
    return flux[None], result


def solution(mesh):
    in_specs = (P("row", None, "ma", None, None), P("ma", None, None), P(), P())
    out_specs = (P("row", "ma", None, None), P("row", None, "ma", None, None))
    return jax.shard_map(local, mesh=mesh, in_specs=in_specs, out_specs=out_specs, check_vma=False)
```

```python
import math

import jax
import jax.numpy as jnp
import numpy as np
from jax import lax
from jax.experimental import pallas as pl
from jax.experimental.pallas import tpu as pltpu
from jax.sharding import PartitionSpec as P

LMAX = 511
NPHI = 1536
NPAIRS = 256
PACK = 513
LANES = 128
TILES = -(-PACK // LANES)
FULL = PACK // LANES * LANES
WIDTH = 256
SCOPED = 16 << 20
LEGENDRE_SCOPED = 56 << 20
SYNTHESIS_SCOPED = 65300 << 10
GROUP = 4
FIRST = 6
BF16 = jnp.bfloat16
F32 = jnp.float32
NT = (((1,), (1,)), ((), ()))


def chebyshev_pair(levels):
    index = np.arange(levels)
    cosines = np.cos(np.pi * (np.outer(index, index) % (2 * (levels - 1))) / (levels - 1))
    ends = np.where((index == 0) | (index == levels - 1), 0.5, 1.0)
    analysis = (2.0 / (levels - 1)) ** 0.5 * np.outer(ends, ends) * cosines
    return cosines.astype(np.float32), analysis.astype(np.float32)


def one_hot(theta):
    half = theta.shape[0]
    natural = lax.broadcasted_iota(jnp.int32, (half, half), 0)
    return jnp.where(natural == theta.reshape(1, half), 1.0, 0.0).astype(BF16)


def slot_masks(pair, column, order_odd):
    used = pair < NPAIRS
    low = jnp.where(used & (column <= LMAX - pair), 1.0, 0.0)
    high = jnp.where(used & (column > LMAX - pair), 1.0, 0.0)
    low_sign = (1 - 2 * (column & 1)).astype(F32)
    high_sign = (1 - 2 * ((column + pair) & 1)).astype(F32)
    return jnp.where(order_odd, high, low), jnp.where(order_odd, high_sign, low_sign)


def slot_copies(source_ref, table_ref, arrived):
    copies = [
        pltpu.make_async_copy(source_ref.at[slot], table_ref.at[slot], arrived.at[slot])
        for slot in range(table_ref.shape[0])
    ]
    for copy in copies[:FIRST]:
        copy.start()
    return copies


def slot_groups(slots):
    return [(0, 2)] + [(s, min(s + GROUP, slots)) for s in range(2, slots, GROUP)]


def synthesis_kernel(
    pairs_ref, source_ref, given_ref, owner_ref, result_ref,
    rows_ref, spectra_ref, theta_ref, here, out_ref, gone, table_ref, arrived,
):
    slots = table_ref.shape[0]
    given = pltpu.make_async_copy(given_ref, spectra_ref, here.at[0])
    owner = pltpu.make_async_copy(owner_ref, theta_ref, here.at[1])
    given.start()
    owner.start()
    copies = slot_copies(source_ref, table_ref, arrived)
    first = lax.axis_index("ma") * slots
    owners = out_ref.shape[0]
    own_half = theta_ref.shape[0] // owners
    groups = rows_ref.shape[0]
    block = 6 * slots
    row = lax.broadcasted_iota(jnp.int32, (8, LANES), 0)
    odd = (row & 1) == 1
    field = row >> 1
    lane = lax.broadcasted_iota(jnp.int32, (8, LANES), 1)

    def left_of(slot):
        pair = pairs_ref[first + slot]
        weight = jnp.where((pair == 0) & (row & 1 == 0), 1.0, 2.0)
        blocks = [[], [], [], []]
        picked = [f * slots + slot for f in range(3)]
        for j in range(TILES):
            if j < TILES - 1:
                tiles = [spectra_ref[i, :, j * LANES : (j + 1) * LANES] for i in picked]
            else:
                tiles = [
                    jnp.broadcast_to(spectra_ref[i, :, FULL:PACK], (2, LANES)) for i in picked
                ]
            mask, sign = slot_masks(pair, lane + j * LANES, odd)
            mask = mask * weight
            for c in range(2):
                parts = [jnp.broadcast_to(t[c : c + 1], (8, LANES)) for t in tiles]
                base = jnp.where(field == 0, parts[0], jnp.where(field == 1, parts[1], parts[2]))
                base = base * mask
                blocks[2 * c].append(base)
                blocks[2 * c + 1].append(base * sign)
        left = jnp.concatenate([jnp.concatenate(b, axis=1) for b in blocks], axis=0)
        return left[:, :FULL].astype(BF16), left[:, FULL : FULL + 1]

    def sums_of(slot, left):
        sums = jnp.dot(left[0], table_ref[slot, :FULL, :], preferred_element_type=F32)
        return sums + left[1] * table_ref[slot, FULL:PACK, :].astype(F32)

    def keep(slot, sums):
        for k in range(4):
            for g in range(groups):
                rows_ref[g, pl.ds(k * block + slot, 6, stride=slots), :] = sums[
                    k * 8 : k * 8 + 6, g * LANES : (g + 1) * LANES
                ]

    given.wait()
    owner.wait()
    for copy in copies[FIRST:]:
        copy.start()
    batches = slot_groups(slots)
    lefts = [left_of(slot) for slot in range(*batches[0])]
    select = one_hot(theta_ref[...])
    done = []
    for number, (start, end) in enumerate(batches):
        for copy in copies[start:end]:
            copy.wait()
        made = [(slot, sums_of(slot, lefts[slot - start])) for slot in range(start, end)]
        if number + 1 < len(batches):
            lefts = [left_of(slot) for slot in range(*batches[number + 1])]
        for slot, sums in done:
            keep(slot, sums)
        done = made
    for slot, sums in done:
        keep(slot, sums)
    moved = []
    for k in range(4):
        rows = jnp.concatenate(
            [rows_ref[g, k * block : (k + 1) * block, :] for g in range(groups)], axis=1
        ).astype(BF16)
        moved.append(jnp.dot(rows, select, preferred_element_type=F32))
    sent = []
    for d in range(owners):
        out_ref[d] = jnp.concatenate(
            [m[:, d * own_half : (d + 1) * own_half] for m in moved], axis=1
        ).astype(BF16)
        sent.append(pltpu.make_async_copy(out_ref.at[d], result_ref.at[d], gone.at[d]))
        sent[-1].start()
    for copy in sent:
        copy.wait()


def table_kernel(
    coarse_cos_ref, coarse_sin_ref, fine_cos_ref, fine_sin_ref, synth_ref, analysis_ref,
    out_ref, kept_synth_ref, kept_analysis_ref,
):
    kept_synth_ref[...] = synth_ref[...]
    kept_analysis_ref[...] = analysis_ref[...]
    rows = fine_cos_ref.shape[0]
    fine_cos = fine_cos_ref[...]
    fine_sin = fine_sin_ref[...]
    for a in range(NPHI // LANES):
        cos_a = coarse_cos_ref[:, a : a + 1]
        sin_a = coarse_sin_ref[:, a : a + 1]
        span = slice(a * LANES, (a + 1) * LANES)
        out_ref[:rows, span] = (cos_a * fine_cos - sin_a * fine_sin).astype(BF16)
        out_ref[rows:, span] = (-(sin_a * fine_cos + cos_a * fine_sin)).astype(BF16)


def scatter_row(wide_ref, row, rows, value):
    wide_ref[pl.ds(row, value.shape[0], stride=rows), :] = value


def scatter_rows(wide_ref, row, rows, values):
    full = values[0].shape[1] // LANES
    for value in values:
        for j in range(full):
            scatter_row(wide_ref, row, rows, value[:, j * LANES : (j + 1) * LANES])
            row += 1
    rest = [value[:, full * LANES :] for value in values]
    filled = sum(r.shape[1] for r in rest)
    rest.append(jnp.zeros((rest[0].shape[0], LANES - filled), F32))
    scatter_row(wide_ref, row, rows, jnp.concatenate(rest, axis=1))
    scatter_row(wide_ref, row + 1, rows, jnp.zeros_like(values[0][:, :LANES]))


def gather_rows(wide_ref, count, rows, arrays, width):
    full = width // LANES
    line = lambda row: wide_ref[pl.ds(row, count, stride=rows), :]
    rest = line(arrays * full)
    part = width - full * LANES
    return [
        jnp.concatenate(
            [line(a * full + j) for j in range(full)] + [rest[:, a * part : (a + 1) * part]],
            axis=1,
        )
        for a in range(arrays)
    ]


def widen(tiles_ref, wide_ref, count, stride, taken):
    for i in range(count):
        for t in range(taken):
            line = 2 * (i * taken + t)
            wide_ref[line : line + 2, :] = tiles_ref[i * stride + t].astype(F32)


def narrow(wide_ref, tiles_ref):
    for t in range(tiles_ref.shape[0]):
        tiles_ref[t] = wide_ref[2 * t : 2 * t + 2, :].astype(BF16)


def turn_kernel(rows_ref, out_ref, wide_ref):
    owners = rows_ref.shape[0]
    part = rows_ref.shape[1] // 3
    theta = rows_ref.shape[2] // 2
    wide = [rows_ref[d].astype(F32) for d in range(owners)]
    lines = []
    for f in range(3):
        turned = jnp.concatenate([w[f * part : (f + 1) * part] for w in wide], axis=0).T
        lines.append(jnp.concatenate([turned[:theta], turned[theta:]], axis=1))
    scatter_rows(wide_ref, 0, wide_ref.shape[0] // theta, lines)
    narrow(wide_ref, out_ref)


def grid_kernel(
    tiles_ref, table_ref, synth_ref, analysis_ref, out_ref, wide_ref, left_ref, both_ref, out_wide_ref
):
    levels = synth_ref.shape[0]
    orders = table_ref.shape[0]
    per_level = tiles_ref.shape[0] // levels
    widen(tiles_ref, wide_ref, levels, per_level, per_level)
    for f, line in enumerate(gather_rows(wide_ref, levels, 2 * per_level, 3, orders)):
        line = line.astype(BF16)
        left_ref[f * levels : (f + 1) * levels, :] = jnp.dot(
            synth_ref[...], jnp.concatenate([line, line], axis=0), preferred_element_type=F32
        ).astype(BF16)
    rows = out_wide_ref.shape[0] // levels
    flux_row = rows - 2 * NPHI // LANES
    for q in range(NPHI // WIDTH):
        span = slice(q * WIDTH, (q + 1) * WIDTH)
        grid = jnp.dot(left_ref[...], table_ref[:, span], preferred_element_type=F32)
        for g in range(2):
            flux = (grid[:levels] * grid[(1 + g) * levels : (2 + g) * levels]).astype(BF16)
            both_ref[g * levels : (g + 1) * levels, span] = flux
            flux = flux.astype(F32)
            for j in range(WIDTH // LANES):
                row = flux_row + 2 * (q * (WIDTH // LANES) + j) + g
                scatter_row(out_wide_ref, row, rows, flux[:, j * LANES : (j + 1) * LANES])
    fourier = lax.dot_general(
        both_ref[...], table_ref[...], NT, preferred_element_type=F32
    ) * NPHI ** (-0.5)
    mixed = []
    for g in range(2):
        value = fourier[g * levels : (g + 1) * levels]
        upper = value.astype(BF16)
        lower = (value - upper.astype(F32)).astype(BF16)
        right = jnp.concatenate([upper, lower, upper], axis=0)
        mixed.append(jnp.dot(analysis_ref[...], right, preferred_element_type=F32))
    scatter_rows(out_wide_ref, 0, rows, mixed)
    narrow(out_wide_ref, out_ref)


def return_kernel(tiles_ref, out_ref, wide_ref, sum_ref):
    owners = out_ref.shape[0]
    part = out_ref.shape[1] // 2
    orders = 2 * owners * part
    theta = out_ref.shape[2] // 2
    taken = wide_ref.shape[0] // (2 * theta)
    widen(tiles_ref, wide_ref, theta, tiles_ref.shape[0] // theta, taken)
    lines = gather_rows(wide_ref, theta, 2 * taken, 2, orders)
    sum_ref[...] = jnp.concatenate(lines, axis=0).T
    for d in range(owners):
        out_ref[d] = jnp.concatenate(
            [
                sum_ref[c * owners * part + d * part : c * owners * part + (d + 1) * part, :]
                for c in range(2)
            ],
            axis=0,
        ).astype(BF16)


def flux_kernel(tiles_ref, out_ref):
    theta = out_ref.shape[0]
    stride = tiles_ref.shape[0] // theta
    count = NPHI // LANES
    for t in range(theta):
        for q in range(count):
            out_ref[t, :, q * LANES : (q + 1) * LANES] = tiles_ref[t * stride + stride - count + q]


def analysis_kernel(
    pairs_ref, source_ref, rows_ref, theta_ref, result_ref,
    nat_ref, out_ref, gone, table_ref, arrived,
):
    slots = table_ref.shape[0]
    copies = slot_copies(source_ref, table_ref, arrived)
    first = lax.axis_index("ma") * slots
    owners = rows_ref.shape[0]
    own_half = theta_ref.shape[0] // owners
    block = rows_ref.shape[1]
    groups = nat_ref.shape[0]
    select = one_hot(theta_ref[...])
    wide = [rows_ref[d].astype(F32) for d in range(owners)]
    for k in range(4):
        own = jnp.concatenate([w[:, k * own_half : (k + 1) * own_half] for w in wide], axis=1)
        nat = lax.dot_general(own.astype(BF16), select, NT, preferred_element_type=F32)
        for g in range(groups):
            nat_ref[g, k * block : (k + 1) * block, :] = nat[:, g * LANES : (g + 1) * LANES]
    for copy in copies[FIRST:]:
        copy.start()
    sent = []
    row = lax.broadcasted_iota(jnp.int32, (16, LANES), 0)
    odd = (row & 1) == 1
    south = (row & 4) == 4
    lane = lax.broadcasted_iota(jnp.int32, (16, LANES), 1)

    def products(slot):
        left = jnp.concatenate(
            [nat_ref[g, pl.ds(slot, 16, stride=slots), :] for g in range(groups)], axis=1
        )
        sums = lax.dot_general(
            left.astype(BF16), table_ref[slot, :FULL, :], NT, preferred_element_type=F32
        )
        last = jnp.sum(left * table_ref[slot, FULL:PACK, :].astype(F32), axis=1, keepdims=True)
        return sums, last

    def finish(slot, sums, last):
        pair = pairs_ref[first + slot]
        for j in range(TILES):
            mask, sign = slot_masks(pair, lane + j * LANES, odd)
            if j < TILES - 1:
                part = sums[:, j * LANES : (j + 1) * LANES]
            else:
                part = jnp.where(lane == 0, last, 0.0)
            part = part * mask * jnp.where(south, sign, 1.0)
            width = min(LANES, PACK - j * LANES)
            for g in range(2):
                both = part[g * 8 : g * 8 + 4] + part[g * 8 + 4 : g * 8 + 8]
                tile = jnp.concatenate([both[0:1] + both[1:2], both[2:3] + both[3:4]], axis=0)
                out_ref[g * slots + slot, :, j * LANES : j * LANES + width] = tile[:, :width]

    def send(number, start, end):
        for g in range(2):
            part = pl.ds(g * slots + start, end - start)
            copy = pltpu.make_async_copy(
                out_ref.at[part], result_ref.at[part], gone.at[2 * number + g]
            )
            copy.start()
            sent.append(copy)

    batches = slot_groups(slots)
    done = []
    for number, (start, end) in enumerate(batches):
        for copy in copies[start:end]:
            copy.wait()
        made = [(slot, *products(slot)) for slot in range(start, end)]
        for values in done:
            finish(*values)
        if number:
            send(number - 1, *batches[number - 1])
        done = made
    for values in done:
        finish(*values)
    send(len(batches) - 1, *batches[-1])
    for copy in sent:
        copy.wait()


def call(kernel, name, out_shape, operands, scratch=(), scalars=0):
    operands = [
        x if i < scalars else pltpu.with_memory_space_constraint(x, pltpu.VMEM)
        for i, x in enumerate(operands)
    ]
    return pl.pallas_call(
        kernel,
        out_shape=tuple(pltpu.VMEM(shape, dtype) for shape, dtype in out_shape),
        in_specs=[
            pl.BlockSpec(memory_space=pltpu.SMEM if i < scalars else pltpu.VMEM)
            for i in range(len(operands))
        ],
        out_specs=(pl.BlockSpec(memory_space=pltpu.VMEM),) * len(out_shape),
        scratch_shapes=scratch,
        compiler_params=pltpu.CompilerParams(vmem_limit_bytes=SCOPED),
        name=name,
    )(*operands)


def two_parts(matrix):
    upper = jnp.asarray(matrix).astype(BF16)
    return upper, (matrix - upper.astype(F32)).astype(BF16)


def trig_table(pair_slots, owners, slot_dev, matrices):
    pairs = pair_slots.reshape(owners, 1, slot_dev)
    orders = jnp.concatenate([pairs, LMAX - pairs], axis=1).reshape(-1, 1)
    span = lax.broadcasted_iota(jnp.int32, (1, LANES), 1)
    coarse = (orders * (span * LANES)) % NPHI
    fine = (orders * span) % NPHI
    scale = 2.0 * math.pi / NPHI
    coarse = coarse.astype(F32) * scale
    fine = fine.astype(F32) * scale
    shape = (2 * orders.shape[0], NPHI)
    trig = (jnp.cos(coarse), jnp.sin(coarse), jnp.cos(fine), jnp.sin(fine))
    made = [(shape, BF16)] + [(m.shape, BF16) for m in matrices]
    return call(table_kernel, "table", made, trig + matrices)


def local(spectra, legendre, pair_slots, theta_owner):
    slot_dev, _, half = legendre.shape
    owners = lax.axis_size("ma")
    levels = lax.axis_size("row") * spectra.shape[0]
    theta_dev = 2 * half // owners
    groups = half // LANES
    synth_upper, synth_lower = two_parts(chebyshev_pair(levels)[0])
    upper, lower = two_parts(chebyshev_pair(levels)[1])
    matrices = (
        jnp.concatenate([synth_upper, synth_lower], axis=1),
        jnp.concatenate([upper, upper, lower], axis=1),
    )
    made = trig_table(pair_slots, owners, slot_dev, matrices)
    orders = made[0].shape[0]

    vmem = pl.BlockSpec(memory_space=pltpu.VMEM)
    smem = pl.BlockSpec(memory_space=pltpu.SMEM)
    far = pl.BlockSpec(memory_space=pltpu.HBM)
    held = [pltpu.VMEM(legendre.shape, BF16), pltpu.SemaphoreType.DMA((slot_dev,))]
    params = pltpu.CompilerParams(vmem_limit_bytes=LEGENDRE_SCOPED)
    near = lambda x: pltpu.with_memory_space_constraint(x, pltpu.VMEM)

    flat = jnp.transpose(spectra, (0, 1, 2, 4, 3)).reshape(3 * slot_dev, 2, PACK)
    outgoing = pl.pallas_call(
        synthesis_kernel,
        out_shape=jax.ShapeDtypeStruct((owners, 6 * slot_dev, LANES), BF16),
        in_specs=[smem, far, far, far],
        out_specs=far,
        scratch_shapes=[
            pltpu.VMEM((groups, 26 * slot_dev + 4, LANES), F32),
            pltpu.VMEM(flat.shape, F32),
            pltpu.VMEM(theta_owner.shape, jnp.int32),
            pltpu.SemaphoreType.DMA((2,)),
            pltpu.VMEM((owners, 6 * slot_dev, LANES), BF16),
            pltpu.SemaphoreType.DMA((owners,)),
        ]
        + held,
        compiler_params=pltpu.CompilerParams(vmem_limit_bytes=SYNTHESIS_SCOPED),
        name="synthesis",
    )(pair_slots, legendre, flat, theta_owner)
    rows = lax.all_to_all(outgoing, "ma", split_axis=0, concat_axis=0, tiled=True)
    rows, made = lax.optimization_barrier((rows, made))

    full, rest = divmod(orders, LANES)
    sent = -(-(3 * full + 1) // 2)
    assert 3 * rest <= LANES and 2 * rest <= LANES and theta_dev == levels
    (tiles,) = call(
        turn_kernel,
        "turn",
        [((theta_dev * sent, 2, LANES), BF16)],
        (rows,),
        [pltpu.VMEM((theta_dev * sent * 2 + 8, LANES), F32)],
    )
    tiles = lax.all_to_all(tiles, "row", split_axis=0, concat_axis=0, tiled=True)
    taken = -(-(2 * full + 1) // 2)
    back = taken + NPHI // LANES
    (tiles,) = call(
        grid_kernel,
        "grid",
        [((levels * back, 2, LANES), BF16)],
        (tiles,) + tuple(made),
        [
            pltpu.VMEM((levels * sent * 2 + 8, LANES), F32),
            pltpu.VMEM((3 * levels, orders), BF16),
            pltpu.VMEM((2 * levels, NPHI), BF16),
            pltpu.VMEM((levels * back * 2 + 8, LANES), F32),
        ],
    )
    tiles = lax.all_to_all(tiles, "row", split_axis=0, concat_axis=0, tiled=True)
    (fourier,) = call(
        return_kernel,
        "return",
        [((owners, 4 * slot_dev, 2 * theta_dev), BF16)],
        (tiles,),
        [
            pltpu.VMEM((theta_dev * taken * 2 + 8, LANES), F32),
            pltpu.VMEM((orders, 2 * theta_dev), F32),
        ],
    )
    flux = pl.pallas_call(
        flux_kernel,
        out_shape=jax.ShapeDtypeStruct((theta_dev, 2, NPHI), BF16),
        in_specs=[vmem],
        compiler_params=pltpu.CompilerParams(vmem_limit_bytes=SCOPED),
        name="flux",
    )(near(tiles))
    returned = lax.all_to_all(fourier, "ma", split_axis=0, concat_axis=0, tiled=True)
    returned, flux = lax.optimization_barrier((returned, flux))
    result = pl.pallas_call(
        analysis_kernel,
        out_shape=jax.ShapeDtypeStruct((2 * slot_dev, 2, PACK), F32),
        in_specs=[smem, far, vmem, vmem],
        out_specs=far,
        scratch_shapes=[
            pltpu.VMEM((groups, 16 * slot_dev, LANES), F32),
            pltpu.VMEM((2 * slot_dev, 2, PACK), F32),
            pltpu.SemaphoreType.DMA((2 * len(slot_groups(slot_dev)),)),
        ]
        + held,
        compiler_params=params,
        name="analysis",
    )(pair_slots, legendre, near(returned), near(theta_owner))
    result = jnp.transpose(result.reshape(1, 2, slot_dev, 2, PACK), (0, 1, 2, 4, 3))
    return flux[None], result


def solution(mesh):
    in_specs = (P("row", None, "ma", None, None), P("ma", None, None), P(), P())
    out_specs = (P("row", "ma", None, None), P("row", None, "ma", None, None))
    return jax.shard_map(local, mesh=mesh, in_specs=in_specs, out_specs=out_specs, check_vma=False)
```
